256 devices in a mesh: atoms: 32 (over z, y_hi, core), kvec: 8 (over y_lo, x).
Axes of the slice: x: 4, y: 4 (y_hi: 2, y_lo: 2; y = y_hi * 2 + y_lo), z: 8, core: 2. Of those that a mesh axis runs over, the one named last changes fastest.
Arguments:
- particle_traits: bfloat16 [131072, 256], P('atoms'), may hold values from -6 to 6
- particle_coordinates: float32 [3, 131072], P(None, 'atoms'), may hold values from 0 to 24
- kspace_vectors: float32 [3, 4096], P(None, 'kvec'), may hold values from -1.5 to 1.5
- learned_kspace_filter: float32 [4096, 256], P('kvec'), may hold values from -4 to 4
- spatial_home: int32 [32, 4096], P('atoms'), may hold values from 0 to 4095, each once within a row
- following_halo_lines: int32 [32, 512], P('atoms'), may hold values from 0 to 4095
- previous_halo_lines: int32 [32, 512], P('atoms'), may hold values from 0 to 4095
- sender_projection: bfloat16 [256, 256], replicated, may hold values from -0.375 to 0.375
- receiver_projection: bfloat16 [256, 256], replicated, may hold values from -0.375 to 0.375
- pair_channel_mapping: bfloat16 [196, 256], replicated, may hold values from -0.375 to 0.375
- vertex_rescaling_gain: float32 [256], replicated, may hold values from 0.1 to 1.9
- link_sender_line: int32 [1048576], P(('atoms', 'kvec')), may hold values from 0 to 5119
- link_receiver_particle: int32 [1048576], P(('atoms', 'kvec')), may hold values from 0 to 4095
- active_link_tally: int32 [256], P(('atoms', 'kvec')), may hold values from 32 to 4096, as said below
Outputs:
- orbital_blocks: bfloat16 [196, 1048576], P(None, ('atoms', 'kvec'))
- partitioned: bfloat16 [131072, 256], P('atoms')
The draws below stay inside these ranges and needn't reach their ends.
Inputs may be any that keep to these rules, and one draw needn't show every extreme that they name: `spatial_home`: each row of destination orders one device's 4096 atoms; every device sends exactly 128 atoms to every partition. `following_halo_lines`: rows of the sending partition. `previous_halo_lines`: rows of the sending partition. `link_sender_line`: A table row: the partition's 4096 own atoms, then 512 ghosts from the previous partition, then 512 from the next. `active_link_tally`: A multiple of 32; the used edges are the first ones of a device's list; some device uses all 4096 slots.
All inputs are finite; a program needn't handle non-finite values.
Results may differ from the reference program's by a relative error of at most 0.01.
Values may be sent and summed in bfloat16 or wider, within the bound.
No kernel may reach another device: no remote copies, remote signals or barrier semaphores. Data moves between devices by JAX's collectives and lax.ppermute only.
A program may use at most 64 MiB of HBM per device.

```python
import math
import jax
import jax.numpy as jnp
from jax import lax

C = 256
KSPACE_NUMBER = 4096
ORB = 196
A_DEV = 4096
E_DEV = 4096
G = 512
GRP = 128
ATOMS = 131072
EDGES = 1048576
N_ATOMS = 32
N_KVEC = 8
DEVICES = 256


def draw_active_link_tally(key, part):
    first_key = jax.random.fold_in(key, 11)
    second_key = jax.random.fold_in(key, 23)
    counts = jax.random.randint(first_key, (DEVICES,), 1, E_DEV // 32 + 1) * 32
    full_dev = jax.random.randint(second_key, (), 0, DEVICES)
    return jnp.where(jnp.arange(DEVICES) == full_dev, E_DEV, counts).astype(jnp.int32)


def plant(result, own_key, least, high):
    longest = result.shape.index(max(result.shape))
    spots = []
    for shift in (0, 1):
        where = [jax.random.randint(jax.random.fold_in(own_key, axis), (), 0, length) for axis, length in enumerate(result.shape)]
        where[longest] = (where[longest] + shift) % result.shape[longest]
        spots.append(tuple(where))
    return result.at[spots[0]].set(least).at[spots[1]].set(high)


def steps_of(key, extent, cuts, smallest, high):
    def one(position, shards_of):
        steps = jax.random.uniform(jax.random.fold_in(jax.random.fold_in(key, 6), position), (shards_of,), jnp.float32, smallest / len(cuts), high / len(cuts))
        return jnp.repeat(jnp.exp(steps), extent[position] // shards_of).reshape((-1,) + (1,) * (len(extent) - position - 1))

    loudness = one(*cuts[0])
    for cut in cuts[1:]:
        loudness = loudness * one(*cut)
    return loudness


def bell_draw(own_key, dims, spread, most, pieces=(), kind=jnp.bfloat16):
    level = steps_of(own_key, dims, pieces, -0.22, 0.18) if pieces else 1.0
    entries = jax.random.normal(own_key, dims, jnp.float32) * spread * level
    return jnp.minimum(jnp.maximum(entries, -most), most).astype(kind)


def setup_inputs(seed: int = 0) -> dict:
    seeds = jax.random.split(jax.random.key(seed), 15)
    return {
        "particle_traits": bell_draw(seeds[0], (ATOMS, C), 1.0, 6.0, ((0, 32),)),
        "particle_coordinates": jnp.clip(24.0 * jax.random.uniform(seeds[1], (3, ATOMS), jnp.float32) ** steps_of(seeds[1], (3, ATOMS), ((1, 32),), -0.2, 0.2), 0.0, 24.0),
        "kspace_vectors": jnp.clip(jax.random.uniform(seeds[2], (3, KSPACE_NUMBER), jnp.float32, -1.5, 1.5) * steps_of(seeds[2], (3, KSPACE_NUMBER), ((1, 8),), -0.4, 0.0), -1.5, 1.5),
        "learned_kspace_filter": bell_draw(seeds[3], (KSPACE_NUMBER, C), 1.0, 4.0, ((0, 8),), jnp.float32),
        "spatial_home": jax.vmap(lambda own: jax.random.permutation(own, A_DEV))(jax.random.split(seeds[4], N_ATOMS)).reshape((N_ATOMS, A_DEV)).astype(jnp.int32),
        "following_halo_lines": plant(jax.random.randint(seeds[5], (N_ATOMS, G), 0, A_DEV), jax.random.fold_in(seeds[5], 1), 0, A_DEV - 1).astype(jnp.int32),
        "previous_halo_lines": plant(jax.random.randint(seeds[6], (N_ATOMS, G), 0, A_DEV), jax.random.fold_in(seeds[6], 1), 0, A_DEV - 1).astype(jnp.int32),
        "sender_projection": bell_draw(seeds[7], (C, C), C ** -0.5, 0.375),
        "receiver_projection": bell_draw(seeds[8], (C, C), C ** -0.5, 0.375),
        "pair_channel_mapping": bell_draw(seeds[9], (ORB, C), C ** -0.5, 0.375),
        "vertex_rescaling_gain": jnp.clip(1.0 + 0.18 * jax.random.normal(seeds[10], (C,), jnp.float32), 0.1, 1.9),
        "link_sender_line": plant(jax.random.randint(seeds[11], (EDGES,), 0, A_DEV + 2 * G), jax.random.fold_in(seeds[11], 1), 0, (A_DEV + 2 * G) - 1).astype(jnp.int32),
        "link_receiver_particle": plant(jax.random.randint(seeds[12], (EDGES,), 0, A_DEV), jax.random.fold_in(seeds[12], 1), 0, A_DEV - 1).astype(jnp.int32),
        "active_link_tally": draw_active_link_tally(jax.random.fold_in(seeds[14], 71), 0),
    }


def reference(particle_traits, particle_coordinates, kspace_vectors, learned_kspace_filter, spatial_home, following_halo_lines, previous_halo_lines, sender_projection, receiver_projection, pair_channel_mapping, vertex_rescaling_gain, link_sender_line, link_receiver_particle, active_link_tally):
    norm_scale = 1.0 / math.sqrt(ATOMS * KSPACE_NUMBER)
    kspace_group = min(512, KSPACE_NUMBER)
    nblocks = KSPACE_NUMBER // kspace_group

    def kspace_stride(summed_increment, kspace_group_number):
        kspace_portion = lax.dynamic_slice_in_dim(kspace_vectors, kspace_group_number * kspace_group, kspace_group, 1)
        filter_portion = lax.dynamic_slice_in_dim(learned_kspace_filter, kspace_group_number * kspace_group, kspace_group, 0)
        wave_arguments = particle_coordinates[0][:, None] * kspace_portion[0][None, :] + particle_coordinates[1][:, None] * kspace_portion[1][None, :]
        wave_arguments = wave_arguments + particle_coordinates[2][:, None] * kspace_portion[2][None, :]
        cosine_vals = jnp.cos(wave_arguments).astype(jnp.bfloat16)
        sine_vals = jnp.sin(wave_arguments).astype(jnp.bfloat16)
        struct_cos = jnp.dot(cosine_vals.T, particle_traits, preferred_element_type=jnp.float32)
        struct_sin = jnp.dot(sine_vals.T, particle_traits, preferred_element_type=jnp.float32)
        filt_cos = (filter_portion * struct_cos * norm_scale).astype(jnp.bfloat16)
        filt_sin = (filter_portion * struct_sin * norm_scale).astype(jnp.bfloat16)
        summed_increment = summed_increment + jnp.dot(cosine_vals, filt_cos, preferred_element_type=jnp.float32)
        summed_increment = summed_increment + jnp.dot(sine_vals, filt_sin, preferred_element_type=jnp.float32)
        return (summed_increment, None)
    summed_increment, _ = lax.scan(kspace_stride, jnp.zeros((ATOMS, C), jnp.float32), jnp.arange(nblocks, dtype=jnp.int32))
    refreshed = particle_traits.astype(jnp.float32) + jax.nn.silu(summed_increment)
    node = (refreshed * lax.rsqrt(lax.optimization_barrier(jnp.mean(refreshed * refreshed, axis=-1, keepdims=True)) + 1e-06) * vertex_rescaling_gain).astype(jnp.bfloat16)
    source_dev = jnp.arange(ATOMS, dtype=jnp.int32) // A_DEV
    slot_ids = spatial_home.reshape(-1).astype(jnp.int32)
    target_rows = slot_ids // GRP * A_DEV + source_dev * GRP + slot_ids % GRP
    partitioned = jnp.zeros((ATOMS, C), jnp.bfloat16).at[target_rows].set(node)
    left_proj = jnp.dot(partitioned, sender_projection, preferred_element_type=jnp.float32).astype(jnp.bfloat16)
    right_proj = jnp.dot(partitioned, receiver_projection, preferred_element_type=jnp.float32).astype(jnp.bfloat16)
    edge_ids = jnp.arange(EDGES, dtype=jnp.int32)
    part_ids = edge_ids // (E_DEV * N_KVEC)
    lower_part = (part_ids - 1) % N_ATOMS
    upper_part = (part_ids + 1) % N_ATOMS
    own_rows = part_ids * A_DEV + link_sender_line
    lower_rows = lower_part * A_DEV + following_halo_lines[lower_part, jnp.clip(link_sender_line - A_DEV, 0, G - 1)]
    upper_rows = upper_part * A_DEV + previous_halo_lines[upper_part, jnp.clip(link_sender_line - A_DEV - G, 0, G - 1)]
    source_rows = jnp.where(link_sender_line < A_DEV, own_rows, jnp.where(link_sender_line < A_DEV + G, lower_rows, upper_rows))
    target_idx = part_ids * A_DEV + link_receiver_particle
    in_use = edge_ids % E_DEV < active_link_tally[edge_ids // E_DEV]

    def expand(packed):
        src_rows, dst_rows, used = packed
        pair = (left_proj[src_rows].astype(jnp.float32) * right_proj[dst_rows].astype(jnp.float32)).astype(jnp.bfloat16)
        orb_block = jnp.dot(pair_channel_mapping, pair.T, preferred_element_type=jnp.float32)
        return jnp.where(used[None, :], orb_block, 0.0).astype(jnp.bfloat16)
    blocks = lax.map(expand, (source_rows.reshape(DEVICES, E_DEV), target_idx.reshape(DEVICES, E_DEV), in_use.reshape(DEVICES, E_DEV)))
    orbital_blocks = jnp.transpose(blocks, (1, 0, 2)).reshape(ORB, EDGES)
    return (orbital_blocks, partitioned)
```

```python
import functools
import math

import jax
import jax.numpy as jnp
from jax import lax
from jax.experimental import pallas as pl
from jax.experimental.pallas import tpu as pltpu
from jax.sharding import Mesh
from jax.sharding import PartitionSpec as P

BF = jnp.bfloat16
F32 = jnp.float32
ATOM_AXES = ("z", "yh", "core")
PLANE_AXES = ("z", "yh")
KV_AXES = ("yl", "x")
TILE = 512
TRIG_ROWS = 16

SIN_TERMS = (
    4.442882919124345,
    -7.30824568650903,
    3.6063542184324517,
    -0.8461116503720991,
    0.10982451642340209,
)
COS_TERMS = (
    1.4142134962552282,
    -6.978850948563795,
    5.739460376906981,
    -1.8835579059858576,
    0.31068802752541236,
)


def cos_sin_of_turns(turns):
    r = turns - jnp.round(turns)
    z = r * r
    u = SIN_TERMS[4] * z + SIN_TERMS[3]
    v = COS_TERMS[4] * z + COS_TERMS[3]
    for term in (2, 1, 0):
        u = u * z + SIN_TERMS[term]
        v = v * z + COS_TERMS[term]
    u = u * r
    return 1.0 - u * u, u * v


def three_parts(values):
    first = values.astype(BF).astype(F32)
    rest = values - first
    second = rest.astype(BF).astype(F32)
    third = (rest - second).astype(BF).astype(F32)
    return first, second, third


def store_atom_parts(parts_ref, coordinates):
    a, b, c = three_parts(coordinates)
    for place, part in enumerate((a, a, a, b, b, c)):
        parts_ref[3 * place : 3 * place + 3, :] = part


def store_kspace_parts(parts_ref, vectors):
    a, b, c = three_parts(vectors * (0.5 / math.pi))
    for place, part in enumerate((a, b, c, a, b, a)):
        parts_ref[3 * place : 3 * place + 3, :] = part


def struct_kernel(coord_ref, kvec_ref, feat_ref, out_ref, apart, kpart, klhs, phase, cosv, sinv, acc):
    step = pl.program_id(0)
    kdev = kvec_ref.shape[1]

    @pl.when(step == 0)
    def _():
        apart[...] = jnp.zeros_like(apart)
        kpart[...] = jnp.zeros_like(kpart)
        store_kspace_parts(kpart, kvec_ref[...])
        klhs[...] = kpart[...].T.astype(BF)
        acc[...] = jnp.zeros_like(acc)

    store_atom_parts(apart, coord_ref[...])
    phase[...] = jnp.dot(klhs[...], apart[...].astype(BF), preferred_element_type=F32)

    def some_rows(i, carry):
        rows = pl.ds(pl.multiple_of(i * TRIG_ROWS, TRIG_ROWS), TRIG_ROWS)
        c, s = cos_sin_of_turns(phase[rows, :])
        cosv[rows, :] = c.astype(BF)
        sinv[rows, :] = s.astype(BF)
        return carry

    lax.fori_loop(0, kdev // TRIG_ROWS, some_rows, 0, unroll=4)
    acc[0] += jnp.dot(cosv[...], feat_ref[...], preferred_element_type=F32)
    acc[1] += jnp.dot(sinv[...], feat_ref[...], preferred_element_type=F32)

    @pl.when(step == pl.num_programs(0) - 1)
    def _():
        pieces = out_ref.shape[0]
        piece = out_ref.shape[2]
        for part in range(2):
            out_ref[:, part] = acc[part].reshape(pieces, piece, -1).astype(BF)


def struct_call(coordinates, vectors, feats, pieces):
    atoms, chans = feats.shape
    kdev = vectors.shape[1]
    return pl.pallas_call(
        struct_kernel,
        out_shape=jax.ShapeDtypeStruct((pieces, 2, kdev // pieces, chans), BF),
        grid=(atoms // TILE,),
        in_specs=[
            pl.BlockSpec((3, TILE), lambda i: (0, i)),
            pl.BlockSpec((3, kdev), lambda i: (0, 0)),
            pl.BlockSpec((TILE, chans), lambda i: (i, 0)),
        ],
        out_specs=pl.BlockSpec((pieces, 2, kdev // pieces, chans), lambda i: (0, 0, 0, 0)),
        scratch_shapes=[
            pltpu.VMEM((128, TILE), F32),
            pltpu.VMEM((128, kdev), F32),
            pltpu.VMEM((kdev, 128), BF),
            pltpu.VMEM((kdev, TILE), F32),
            pltpu.VMEM((kdev, TILE), BF),
            pltpu.VMEM((kdev, TILE), BF),
            pltpu.VMEM((2, kdev, chans), F32),
        ],
        cost_estimate=pl.CostEstimate(flops=6 * atoms * kdev * chans, transcendentals=0, bytes_accessed=4 << 20),
        name="struct",
    )(coordinates, vectors, feats)


def waves_kernel(place_ref, coord_ref, kvec_ref, want_ref, feat_ref, waves_ref, picked_ref, apart, kpart, krhs, rows, ordered, phase, acc):
    step = pl.program_id(0)
    atoms = coord_ref.shape[1]
    kdev = kvec_ref.shape[1]

    @pl.when(step == 0)
    def _():
        apart[...] = jnp.zeros_like(apart)
        kpart[...] = jnp.zeros_like(kpart)
        store_kspace_parts(kpart, kvec_ref[...])
        krhs[...] = kpart[...].astype(BF)
        acc[...] = jnp.zeros_like(acc)
        for part in range(atoms // TILE):
            span = slice(part * TILE, (part + 1) * TILE)
            store_atom_parts(apart, coord_ref[:, span])
            rows[span, :] = apart[...].T

        def move(i, carry):
            base = i * 16
            for j in range(16):
                ordered[pl.ds(place_ref[base + j], 1), :] = rows[pl.ds(base + j, 1), :]
            return carry

        lax.fori_loop(0, atoms // 16, move, 0)

    here = pl.ds(pl.multiple_of(step * TILE, TILE), TILE)
    phase[...] = jnp.dot(ordered[here, :].astype(BF), krhs[...], preferred_element_type=F32)

    def some_rows(i, carry):
        span = pl.ds(pl.multiple_of(i * TRIG_ROWS, TRIG_ROWS), TRIG_ROWS)
        c, s = cos_sin_of_turns(phase[span, :])
        waves_ref[span, :kdev] = c.astype(BF)
        waves_ref[span, kdev:] = s.astype(BF)
        return carry

    lax.fori_loop(0, TILE // TRIG_ROWS, some_rows, 0, unroll=4)

    wanted = acc.shape[0]
    hot = lax.broadcasted_iota(jnp.int32, (wanted, TILE), 0) == want_ref[...]
    acc[...] += jnp.dot(
        jnp.where(hot, 1.0, 0.0).astype(BF), feat_ref[...], preferred_element_type=F32
    )

    @pl.when(step == pl.num_programs(0) - 1)
    def _():
        picked_ref[...] = acc[...].astype(BF)


def waves_call(places, want, coordinates, vectors, feats, wanted):
    atoms, chans = feats.shape
    kdev = vectors.shape[1]
    return pl.pallas_call(
        waves_kernel,
        out_shape=(
            jax.ShapeDtypeStruct((atoms, 2 * kdev), BF),
            jax.ShapeDtypeStruct((wanted, chans), BF),
        ),
        grid_spec=pltpu.PrefetchScalarGridSpec(
            num_scalar_prefetch=1,
            grid=(atoms // TILE,),
            in_specs=[
                pl.BlockSpec((3, atoms), lambda i, p: (0, 0)),
                pl.BlockSpec((3, kdev), lambda i, p: (0, 0)),
                pl.BlockSpec((1, TILE), lambda i, p: (0, i)),
                pl.BlockSpec((TILE, chans), lambda i, p: (i, 0)),
            ],
            out_specs=(
                pl.BlockSpec((TILE, 2 * kdev), lambda i, p: (i, 0)),
                pl.BlockSpec((wanted, chans), lambda i, p: (0, 0)),
            ),
            scratch_shapes=[
                pltpu.VMEM((128, TILE), F32),
                pltpu.VMEM((128, kdev), F32),
                pltpu.VMEM((128, kdev), BF),
                pltpu.VMEM((atoms, 128), F32),
                pltpu.VMEM((atoms, 128), F32),
                pltpu.VMEM((TILE, kdev), F32),
                pltpu.VMEM((wanted, chans), F32),
            ],
        ),
        cost_estimate=pl.CostEstimate(flops=4 * atoms * kdev * chans, transcendentals=0, bytes_accessed=12 << 20),
        name="waves",
    )(places, coordinates, vectors, want, feats)


def update_kernel(waves_ref, filt_ref, out_ref, filt):
    kdev = filt.shape[0] // 2

    @pl.when(pl.program_id(0) == 0)
    def _():
        for part in range(2):
            filt[part * kdev : (part + 1) * kdev, :] = filt_ref[:, part].reshape(kdev, -1)

    out_ref[...] = jnp.dot(waves_ref[...], filt[...], preferred_element_type=F32).astype(BF)


def update_call(waves, filtered):
    atoms, columns = waves.shape
    chans = filtered.shape[-1]
    return pl.pallas_call(
        update_kernel,
        out_shape=jax.ShapeDtypeStruct((atoms, chans), BF),
        grid=(atoms // TILE,),
        in_specs=[
            pl.BlockSpec((TILE, columns), lambda i: (i, 0)),
            pl.BlockSpec(filtered.shape, lambda i: (0, 0, 0, 0)),
        ],
        out_specs=pl.BlockSpec((TILE, chans), lambda i: (i, 0)),
        scratch_shapes=[pltpu.VMEM((columns, chans), BF)],
        cost_estimate=pl.CostEstimate(flops=2 * atoms * columns * chans, transcendentals=0, bytes_accessed=11 << 20),
        name="update",
    )(waves, filtered)


def node_kernel(parts_ref, feat_ref, gain_ref, out_ref):
    update = parts_ref[0].astype(F32)
    for part in range(1, parts_ref.shape[0]):
        update = update + parts_ref[part].astype(F32)
    refreshed = feat_ref[...].astype(F32) + update / (1.0 + jnp.exp(-update))
    mean = jnp.mean(refreshed * refreshed, axis=-1, keepdims=True)
    out_ref[...] = (refreshed * lax.rsqrt(mean + 1e-06) * gain_ref[...]).astype(BF)


def node_call(parts, feats, gain):
    count, rows, chans = parts.shape
    block = 128
    return pl.pallas_call(
        node_kernel,
        out_shape=jax.ShapeDtypeStruct((rows, chans), BF),
        grid=(rows // block,),
        in_specs=[
            pl.BlockSpec((count, block, chans), lambda i: (0, i, 0)),
            pl.BlockSpec((block, chans), lambda i: (i, 0)),
            pl.BlockSpec((1, chans), lambda i: (0, 0)),
        ],
        out_specs=pl.BlockSpec((block, chans), lambda i: (i, 0)),
        cost_estimate=pl.CostEstimate(flops=20 * rows * chans, transcendentals=rows * chans, bytes_accessed=3 << 20),
        name="node",
    )(parts, feats, gain)


def relay_kernel(rows_ref, ids_ref, out_ref, halo_ref, acc):
    step = pl.program_id(0)
    here = jnp.swapaxes(rows_ref[...], 0, 1).reshape(out_ref.shape)
    out_ref[...] = here
    tile = out_ref.shape[0]
    hot = lax.broadcasted_iota(jnp.int32, (1, tile), 1) == ids_ref[...] - step * tile
    got = jnp.dot(jnp.where(hot, 1.0, 0.0).astype(BF), here, preferred_element_type=F32)

    @pl.when(step == 0)
    def _():
        acc[...] = got

    @pl.when(step > 0)
    def _():
        acc[...] += got

    @pl.when(step == pl.num_programs(0) - 1)
    def _():
        halo_ref[...] = acc[...].astype(BF)


def relay_call(rows, ids):
    groups, sources, per, chans = rows.shape
    tiles = 8
    halo = ids.shape[0]
    atoms = groups * sources * per
    return pl.pallas_call(
        relay_kernel,
        out_shape=(
            jax.ShapeDtypeStruct((atoms, chans), BF),
            jax.ShapeDtypeStruct((halo, chans), BF),
        ),
        grid=(tiles,),
        in_specs=[
            pl.BlockSpec((groups, sources // tiles, per, chans), lambda i: (0, i, 0, 0)),
            pl.BlockSpec((halo, 1), lambda i: (0, 0)),
        ],
        out_specs=(
            pl.BlockSpec((atoms // tiles, chans), lambda i: (i, 0)),
            pl.BlockSpec((halo, chans), lambda i: (0, 0)),
        ),
        scratch_shapes=[pltpu.VMEM((halo, chans), F32)],
        cost_estimate=pl.CostEstimate(flops=2 * halo * atoms * chans, transcendentals=0, bytes_accessed=5 << 20),
        name="relay",
    )(rows, ids)


def edges_kernel(src_ref, dst_ref, count_ref, own_ref, lower_ref, upper_ref, wl_ref, wr_ref, map_ref, out_ref, left, right, pair):
    step = pl.program_id(0)
    atoms = own_ref.shape[0]
    ghosts = lower_ref.shape[0]

    def project(rows, weight_ref, table, at):
        count = rows.shape[0]
        got = jnp.dot(rows, weight_ref[...], preferred_element_type=F32).astype(BF).astype(F32)
        for half in range(2):
            table[pl.ds(2 * at + half, count, stride=2), :] = got[:, half * 128 : half * 128 + 128]

    @pl.when(step == 0)
    def _():
        for part in range(atoms // TILE):
            rows = own_ref[part * TILE : (part + 1) * TILE, :]
            project(rows, wl_ref, left, part * TILE)
            project(rows, wr_ref, right, part * TILE)
        project(lower_ref[...], wl_ref, left, atoms)
        project(upper_ref[...], wl_ref, left, atoms + ghosts)

    block = out_ref.shape[1]

    def some_edges(i, carry):
        base = i * 16
        for j in range(16):
            at = step * block + base + j
            a = left[pl.ds(pl.multiple_of(src_ref[at] * 2, 2), 2), :]
            b = right[pl.ds(pl.multiple_of(dst_ref[at] * 2, 2), 2), :]
            pair[pl.ds(pl.multiple_of((base + j) * 2, 2), 2), :] = a * b
        return carry

    lax.fori_loop(0, block // 16, some_edges, 0)
    total = None
    for half in range(2):
        value = pair[pl.ds(half, block, stride=2), :].astype(BF)
        part = lax.dot_general(
            map_ref[:, half * 128 : half * 128 + 128],
            value,
            (((1,), (1,)), ((), ())),
            preferred_element_type=F32,
        )
        total = part if total is None else total + part
    at = step * block + lax.broadcasted_iota(jnp.int32, (1, block), 1)
    out_ref[...] = jnp.where(at < count_ref[0], total, 0.0).astype(BF)


def edges_call(src, dst, count, own, lower, upper, wl, wr, mapping):
    atoms, chans = own.shape
    ghosts = lower.shape[0]
    edges = src.shape[0]
    orb = mapping.shape[0]
    whole = lambda a: pl.BlockSpec(a.shape, lambda i, *_: (0, 0))
    return pl.pallas_call(
        edges_kernel,
        out_shape=jax.ShapeDtypeStruct((orb, edges), BF),
        grid_spec=pltpu.PrefetchScalarGridSpec(
            num_scalar_prefetch=3,
            grid=(edges // TILE,),
            in_specs=[whole(a) for a in (own, lower, upper, wl, wr, mapping)],
            out_specs=pl.BlockSpec((orb, TILE), lambda i, *_: (0, i)),
            scratch_shapes=[
                pltpu.VMEM((2 * (atoms + 2 * ghosts), 128), F32),
                pltpu.VMEM((2 * atoms, 128), F32),
                pltpu.VMEM((2 * TILE, 128), F32),
            ],
        ),
        cost_estimate=pl.CostEstimate(flops=2 * edges * chans * orb, transcendentals=0, bytes_accessed=8 << 20),
        name="edges",
    )(src, dst, count, own, lower, upper, wl, wr, mapping)


def exchange(pieces, axes):
    return lax.all_to_all(pieces, axes, 0, 0, tiled=True)


def gather_over(piece, axes):
    copies = lax.axis_size(axes)
    return exchange(jnp.broadcast_to(piece[None], (copies,) + piece.shape), axes)


def local(
    particle_traits,
    particle_coordinates,
    kspace_vectors,
    learned_kspace_filter,
    spatial_home,
    following_halo_lines,
    previous_halo_lines,
    sender_projection,
    receiver_projection,
    pair_channel_mapping,
    vertex_rescaling_gain,
    link_sender_line,
    link_receiver_particle,
    active_link_tally,
):
    n_atoms = lax.axis_size(ATOM_AXES)
    n_planes = lax.axis_size(PLANE_AXES)
    n_cores = lax.axis_size("core")
    n_kvec = lax.axis_size(KV_AXES)
    atoms, chans = particle_traits.shape
    kdev = kspace_vectors.shape[1]
    norm_scale = 1.0 / math.sqrt(atoms * n_atoms * kdev * n_kvec)
    share = atoms // n_kvec
    run = atoms // n_atoms // n_kvec
    piece = kdev // n_atoms

    partial = struct_call(particle_coordinates, kspace_vectors, particle_traits, n_atoms)
    partial = partial.reshape(n_cores, n_planes, 2, piece, chans)
    halves = exchange(partial, "core")
    chip = jnp.sum(halves.astype(F32), axis=0).astype(BF)
    spread = exchange(chip, PLANE_AXES)

    home = spatial_home[0]
    places = (home // run % n_kvec) * share + home // (run * n_kvec) * run + home % run
    want = (places - lax.axis_index(KV_AXES) * share)[None, :]
    waves, feats = waves_call(
        places, want, particle_coordinates, kspace_vectors, particle_traits, share
    )

    struct = jnp.sum(spread.astype(F32), axis=0)
    at = (lax.axis_index("core") * n_planes + lax.axis_index(PLANE_AXES)) * piece
    filter_piece = lax.dynamic_slice_in_dim(learned_kspace_filter, at, piece, 0)
    filtered = (filter_piece[None] * struct * norm_scale).astype(BF)
    filtered = gather_over(filtered, PLANE_AXES)
    filtered = lax.all_gather(filtered, "core", axis=0, tiled=True)

    update = update_call(waves, filtered)
    parts = exchange(update.reshape(n_kvec, share, chans), KV_AXES)
    node = node_call(parts, feats, vertex_rescaling_gain[None, :])
    arrived = exchange(node.reshape(n_atoms, run, chans), ATOM_AXES)
    everything = gather_over(arrived, KV_AXES)
    ids = jnp.concatenate([following_halo_lines[0], previous_halo_lines[0]])[:, None]
    partition_rows, halo = relay_call(everything.reshape(n_kvec, n_atoms, run, chans), ids)
    ghosts = following_halo_lines.shape[1]
    up = [(i, (i + 1) % n_atoms) for i in range(n_atoms)]
    down = [(i, (i - 1) % n_atoms) for i in range(n_atoms)]
    lower = lax.ppermute(halo[:ghosts], ATOM_AXES, up)
    upper = lax.ppermute(halo[ghosts:], ATOM_AXES, down)
    orbital_blocks = edges_call(
        link_sender_line,
        link_receiver_particle,
        active_link_tally,
        partition_rows,
        lower,
        upper,
        sender_projection,
        receiver_projection,
        pair_channel_mapping,
    )
    return (orbital_blocks, partition_rows)


def solution(mesh):
    fine = Mesh(mesh.devices.reshape(8, 2, 2, 2, 4), ATOM_AXES + KV_AXES)
    every = ATOM_AXES + KV_AXES
    placed = (
        P(ATOM_AXES, None),
        P(None, ATOM_AXES),
        P(None, KV_AXES),
        P(KV_AXES, None),
        P(ATOM_AXES, None),
        P(ATOM_AXES, None),
        P(ATOM_AXES, None),
        P(),
        P(),
        P(),
        P(),
        P(every),
        P(every),
        P(every),
    )
    return jax.shard_map(
        local,
        mesh=fine,
        in_specs=placed,
        out_specs=(P(None, every), P(ATOM_AXES, None)),
        check_vma=False,
    )
```

```python
import functools
import math

import jax
import jax.numpy as jnp
from jax import lax
from jax.experimental import pallas as pl
from jax.experimental.pallas import tpu as pltpu
from jax.sharding import Mesh
from jax.sharding import PartitionSpec as P


BF = jnp.bfloat16
F32 = jnp.float32
ATOM_AXES = ("z", "yh", "core")
PLANE_AXES = ("z", "yh")
KV_AXES = ("yl", "x")
TILE = 512
TRIG_ROWS = 16

SIN_TERMS = (
    4.442882919124345,
    -7.30824568650903,
    3.6063542184324517,
    -0.8461116503720991,
    0.10982451642340209,
)
COS_TERMS = (
    1.4142134962552282,
    -6.978850948563795,
    5.739460376906981,
    -1.8835579059858576,
    0.31068802752541236,
)


def cos_sin_of_turns(turns):
    r = turns - jnp.round(turns)
    z = r * r
    u = SIN_TERMS[4] * z + SIN_TERMS[3]
    v = COS_TERMS[4] * z + COS_TERMS[3]
    for term in (2, 1, 0):
        u = u * z + SIN_TERMS[term]
        v = v * z + COS_TERMS[term]
    u = u * r
    return 1.0 - u * u, u * v


def three_parts(values):
    first = values.astype(BF).astype(F32)
    rest = values - first
    second = rest.astype(BF).astype(F32)
    third = (rest - second).astype(BF).astype(F32)
    return first, second, third


def store_atom_parts(parts_ref, coordinates):
    a, b, c = three_parts(coordinates)
    for place, part in enumerate((a, a, a, b, b, c)):
        parts_ref[3 * place : 3 * place + 3, :] = part


def store_kspace_parts(parts_ref, vectors):
    a, b, c = three_parts(vectors * (0.5 / math.pi))
    for place, part in enumerate((a, b, c, a, b, a)):
        parts_ref[3 * place : 3 * place + 3, :] = part


def own_first(vectors, core):
    half = vectors.shape[1] // 2
    a, b = vectors[:, :half], vectors[:, half:]
    first = core == 0
    return jnp.concatenate([jnp.where(first, a, b), jnp.where(first, b, a)], axis=1)


def params(megabytes):
    return pltpu.CompilerParams(vmem_limit_bytes=megabytes << 20)


def struct_kernel(core_ref, coord_ref, kvec_ref, feat_ref, keep_ref, send_ref, apart, kpart, klhs, phase, cosv, sinv, acc):
    step = pl.program_id(0)
    kdev = kvec_ref.shape[1]

    @pl.when(step == 0)
    def _():
        apart[...] = jnp.zeros_like(apart)
        kpart[...] = jnp.zeros_like(kpart)
        store_kspace_parts(kpart, own_first(kvec_ref[...], core_ref[0]))
        klhs[...] = kpart[...].T.astype(BF)
        acc[...] = jnp.zeros_like(acc)

    store_atom_parts(apart, coord_ref[...])
    phase[...] = jnp.dot(klhs[...], apart[...].astype(BF), preferred_element_type=F32)

    def some_rows(i, carry):
        rows = pl.ds(pl.multiple_of(i * TRIG_ROWS, TRIG_ROWS), TRIG_ROWS)
        c, s = cos_sin_of_turns(phase[rows, :])
        cosv[rows, :] = c.astype(BF)
        sinv[rows, :] = s.astype(BF)
        return carry

    lax.fori_loop(0, kdev // TRIG_ROWS, some_rows, 0, unroll=4)
    acc[0] += jnp.dot(cosv[...], feat_ref[...], preferred_element_type=F32)
    acc[1] += jnp.dot(sinv[...], feat_ref[...], preferred_element_type=F32)

    @pl.when(step == pl.num_programs(0) - 1)
    def _():
        planes, _, piece, chans = keep_ref.shape
        half = kdev // 2
        for part in range(2):
            keep_ref[:, part] = acc[part, :half].reshape(planes, piece, chans).astype(BF)
            send_ref[:, part] = acc[part, half:].reshape(planes, piece, chans).astype(BF)


def struct_call(core, coordinates, vectors, feats, planes):
    atoms, chans = feats.shape
    kdev = vectors.shape[1]
    shape = (planes, 2, kdev // 2 // planes, chans)
    return pl.pallas_call(
        struct_kernel,
        out_shape=[jax.ShapeDtypeStruct(shape, BF)] * 2,
        grid_spec=pltpu.PrefetchScalarGridSpec(
            num_scalar_prefetch=1,
            grid=(atoms // TILE,),
            in_specs=[
                pl.BlockSpec((3, TILE), lambda i, c: (0, i)),
                pl.BlockSpec((3, kdev), lambda i, c: (0, 0)),
                pl.BlockSpec((TILE, chans), lambda i, c: (i, 0)),
            ],
            out_specs=[pl.BlockSpec(shape, lambda i, c: (0, 0, 0, 0))] * 2,
            scratch_shapes=[
                pltpu.VMEM((128, TILE), F32),
                pltpu.VMEM((128, kdev), F32),
                pltpu.VMEM((kdev, 128), BF),
                pltpu.VMEM((kdev, TILE), F32),
                pltpu.VMEM((kdev, TILE), BF),
                pltpu.VMEM((kdev, TILE), BF),
                pltpu.VMEM((2, kdev, chans), F32),
            ],
        ),
        compiler_params=params(16),
        cost_estimate=pl.CostEstimate(flops=6 * atoms * kdev * chans, transcendentals=0, bytes_accessed=4 << 20),
        name="struct",
    )(core, coordinates, vectors, feats)


def order_kernel(place_ref, core_ref, coord_ref, kvec_ref, want_ref, feat_ref, ordered_ref, krhs_ref, picked_ref, apart, kpart, rows, ordered, acc):
    atoms = coord_ref.shape[1]
    wanted = picked_ref.shape[0]
    apart[...] = jnp.zeros_like(apart)
    kpart[...] = jnp.zeros_like(kpart)
    store_kspace_parts(kpart, own_first(kvec_ref[...], core_ref[0]))
    krhs_ref[...] = kpart[...].astype(BF)
    for part in range(atoms // TILE):
        span = slice(part * TILE, (part + 1) * TILE)
        store_atom_parts(apart, coord_ref[:, span])
        rows[span, :] = apart[...].T

    def move(i, carry):
        base = i * 32
        for j in range(32):
            ordered[pl.ds(place_ref[base + j], 1), :] = rows[pl.ds(base + j, 1), :]
        return carry

    lax.fori_loop(0, atoms // 32, move, 0)
    acc[...] = jnp.zeros_like(acc)

    def pick(i, carry):
        span = pl.ds(pl.multiple_of(i * TILE, TILE), TILE)
        ordered_ref[span, :] = ordered[span, :].astype(BF)
        hot = lax.broadcasted_iota(jnp.int32, (wanted, TILE), 0) == want_ref[:, span]
        acc[...] += jnp.dot(
            jnp.where(hot, 1.0, 0.0).astype(BF), feat_ref[span, :], preferred_element_type=F32
        )
        return carry

    lax.fori_loop(0, atoms // TILE, pick, 0)
    picked_ref[...] = acc[...].astype(BF)


def order_call(places, want, core, coordinates, vectors, feats, wanted):
    atoms, chans = feats.shape
    kdev = vectors.shape[1]
    whole = pl.BlockSpec(memory_space=pltpu.VMEM)
    return pl.pallas_call(
        order_kernel,
        out_shape=(
            jax.ShapeDtypeStruct((atoms, 128), BF),
            jax.ShapeDtypeStruct((128, kdev), BF),
            jax.ShapeDtypeStruct((wanted, chans), BF),
        ),
        grid_spec=pltpu.PrefetchScalarGridSpec(
            num_scalar_prefetch=2,
            grid=(),
            in_specs=[whole] * 4,
            out_specs=(whole,) * 3,
            scratch_shapes=[
                pltpu.VMEM((128, TILE), F32),
                pltpu.VMEM((128, kdev), F32),
                pltpu.VMEM((atoms, 128), F32),
                pltpu.VMEM((atoms, 128), F32),
                pltpu.VMEM((wanted, chans), F32),
            ],
        ),
        compiler_params=params(16),
        cost_estimate=pl.CostEstimate(flops=4 * atoms * kdev * chans, transcendentals=0, bytes_accessed=12 << 20),
        name="order",
    )(places, core, coordinates, vectors, want, feats)


def update_kernel(rows_ref, krhs_ref, own_ref, other_ref, out_ref, phase, cosv, sinv):
    kdev = krhs_ref.shape[1]
    half = kdev // 2
    phase[...] = jnp.dot(rows_ref[...], krhs_ref[...], preferred_element_type=F32)

    def some_rows(i, carry):
        span = pl.ds(pl.multiple_of(i * TRIG_ROWS, TRIG_ROWS), TRIG_ROWS)
        c, s = cos_sin_of_turns(phase[span, :])
        cosv[span, :] = c.astype(BF)
        sinv[span, :] = s.astype(BF)
        return carry

    lax.fori_loop(0, rows_ref.shape[0] // TRIG_ROWS, some_rows, 0, unroll=4)
    total = None
    for part, wave in enumerate((cosv, sinv)):
        for place, ref in enumerate((own_ref, other_ref)):
            weights = ref[:, part].reshape(half, -1)
            got = jnp.dot(wave[:, place * half : (place + 1) * half], weights, preferred_element_type=F32)
            total = got if total is None else total + got
    out_ref[...] = total.astype(BF)


def update_call(tile, ordered, krhs, own, other):
    kdev = krhs.shape[1]
    chans = own.shape[-1]
    whole = lambda a: pl.BlockSpec(a.shape, lambda i: (0,) * a.ndim)
    return pl.pallas_call(
        update_kernel,
        out_shape=jax.ShapeDtypeStruct((TILE, chans), BF),
        grid=(1,),
        in_specs=[pl.BlockSpec((TILE, 128), lambda i: (tile, 0)), whole(krhs), whole(own), whole(other)],
        out_specs=pl.BlockSpec((TILE, chans), lambda i: (0, 0)),
        scratch_shapes=[
            pltpu.VMEM((TILE, kdev), F32),
            pltpu.VMEM((TILE, kdev), BF),
            pltpu.VMEM((TILE, kdev), BF),
        ],
        compiler_params=params(12),
        cost_estimate=pl.CostEstimate(flops=4 * TILE * kdev * chans, transcendentals=0, bytes_accessed=1 << 20),
        name="update",
    )(ordered, krhs, own, other)


def node_kernel(*refs):
    *part_refs, feat_ref, gain_ref, out_ref = refs
    update = part_refs[0][...].astype(F32)
    for ref in part_refs[1:]:
        update = update + ref[...].astype(F32)
    refreshed = feat_ref[...].astype(F32) + update / (1.0 + jnp.exp(-update))
    mean = jnp.mean(refreshed * refreshed, axis=-1, keepdims=True)
    out_ref[...] = (refreshed * lax.rsqrt(mean + 1e-06) * gain_ref[...]).astype(BF)


def node_call(parts, feats, gain):
    rows, chans = feats.shape
    block = 256
    tile = pl.BlockSpec((block, chans), lambda i: (i, 0))
    return pl.pallas_call(
        node_kernel,
        out_shape=jax.ShapeDtypeStruct((rows, chans), BF),
        grid=(rows // block,),
        in_specs=[tile] * (len(parts) + 1) + [pl.BlockSpec((1, chans), lambda i: (0, 0))],
        out_specs=tile,
        compiler_params=params(8),
        cost_estimate=pl.CostEstimate(flops=20 * rows * chans, transcendentals=rows * chans, bytes_accessed=3 << 20),
        name="node",
    )(*parts, feats, gain)


def pairs_of(piece_refs):
    for kv, refs in enumerate(piece_refs):
        at = 0
        for ref in refs:
            yield kv, at, ref
            at += ref.shape[0]


def store_rows(table, value, starts, run):
    for place, start in enumerate(starts):
        for half in range(2):
            table[pl.ds(start + half, run, stride=2), :] = value[
                place * run : (place + 1) * run, half * 128 : half * 128 + 128
            ]


def project_pieces(piece_refs, kv_ref, weight_ref, table, spots):
    for kv, at, ref in pairs_of(piece_refs):
        count, run, chans = ref.shape
        rows = ref[...].reshape(count * run, chans)
        got = jnp.dot(rows, weight_ref[...], preferred_element_type=F32).astype(BF).astype(F32)
        base = pl.multiple_of(kv_ref[kv] * (2 * run), 2 * run)
        starts = [base + (at + s) * (2 * run * spots) for s in range(count)]
        store_rows(table, got, starts, run)


def halo_kernel(split, kv_ref, ids_ref, *refs):
    flat, (weight_ref, left_ref, down_ref, up_ref, picked) = refs[: sum(split)], refs[sum(split) :]
    pieces, at = [], 0
    for count in split:
        pieces.append(flat[at : at + count])
        at += count
    project_pieces(pieces, kv_ref, weight_ref, left_ref, len(split))
    halo = ids_ref.shape[0]

    def move(i, carry):
        base = i * 32
        for j in range(32):
            row = left_ref[pl.ds(pl.multiple_of(ids_ref[base + j], 2), 2), :]
            picked[pl.ds(pl.multiple_of((base + j) * 2, 2), 2), :] = row
        return carry

    lax.fori_loop(0, halo // 32, move, 0)
    for side, ref in enumerate((down_ref, up_ref)):
        for half in range(2):
            rows = picked[pl.ds(side * halo + half, halo // 2, stride=2), :]
            ref[:, half * 128 : half * 128 + 128] = rows.astype(BF)


def halo_call(pieces, kvs, ids, weight):
    split = tuple(len(p) for p in pieces)
    flat = [a for p in pieces for a in p]
    chans = weight.shape[0]
    halo = ids.shape[0]
    rows = sum(a.shape[0] * a.shape[1] for a in flat)
    whole = pl.BlockSpec(memory_space=pltpu.VMEM)
    return pl.pallas_call(
        functools.partial(halo_kernel, split),
        out_shape=(
            jax.ShapeDtypeStruct((2 * rows, 128), F32),
            jax.ShapeDtypeStruct((halo // 2, chans), BF),
            jax.ShapeDtypeStruct((halo // 2, chans), BF),
        ),
        grid_spec=pltpu.PrefetchScalarGridSpec(
            num_scalar_prefetch=2,
            grid=(),
            in_specs=[whole] * (len(flat) + 1),
            out_specs=(whole,) * 3,
            scratch_shapes=[pltpu.VMEM((2 * halo, 128), F32)],
        ),
        compiler_params=params(16),
        cost_estimate=pl.CostEstimate(flops=2 * rows * chans * chans, transcendentals=0, bytes_accessed=8 << 20),
        name="halo",
    )(kvs, ids, *flat, weight)


def right_kernel(split, kv_ref, dst_ref, *refs):
    flat, (weight_ref, out_ref, got_ref, table) = refs[: sum(split)], refs[sum(split) :]
    pieces, at = [], 0
    for count in split:
        pieces.append(flat[at : at + count])
        at += count
    for kv, at, ref in pairs_of(pieces):
        out_ref[at : at + ref.shape[0], kv_ref[kv]] = ref[...]
    project_pieces(pieces, kv_ref, weight_ref, table, len(split))

    def move(i, carry):
        base = i * 32
        for j in range(32):
            row = table[pl.ds(pl.multiple_of(dst_ref[base + j], 2), 2), :]
            got_ref[pl.ds(pl.multiple_of((base + j) * 2, 2), 2), :] = row
        return carry

    lax.fori_loop(0, dst_ref.shape[0] // 32, move, 0)


def right_call(pieces, kvs, dst, weight):
    split = tuple(len(p) for p in pieces)
    flat = [a for p in pieces for a in p]
    count, run, chans = pieces[0][0].shape
    edges = dst.shape[0]
    rows = sum(a.shape[0] * a.shape[1] for a in flat)
    whole = pl.BlockSpec(memory_space=pltpu.VMEM)
    return pl.pallas_call(
        functools.partial(right_kernel, split),
        out_shape=(
            jax.ShapeDtypeStruct((count, len(split), run, chans), BF),
            jax.ShapeDtypeStruct((2 * edges, 128), F32),
        ),
        grid_spec=pltpu.PrefetchScalarGridSpec(
            num_scalar_prefetch=2,
            grid=(),
            in_specs=[whole] * (len(flat) + 1),
            out_specs=(whole,) * 2,
            scratch_shapes=[pltpu.VMEM((2 * rows, 128), F32)],
        ),
        compiler_params=params(20),
        cost_estimate=pl.CostEstimate(flops=2 * rows * chans * chans, transcendentals=0, bytes_accessed=8 << 20),
        name="right",
    )(kvs, dst, *flat, weight)


def edges_kernel(src_ref, count_ref, left_ref, lower_ref, upper_ref, got_ref, map_ref, out_ref, table, pair):
    step = pl.program_id(0)
    own = left_ref.shape[0]
    ghosts = lower_ref.shape[0]
    block = out_ref.shape[1]

    @pl.when(step == 0)
    def _():
        table[:own, :] = left_ref[...]
        for side, ref in enumerate((lower_ref, upper_ref)):
            value = ref[...].astype(F32)
            store_rows(table, value, [own + side * 2 * ghosts], ghosts)

    def some_edges(i, carry):
        base = i * 32
        for j in range(32):
            at = step * block + base + j
            a = table[pl.ds(pl.multiple_of(src_ref[at], 2), 2), :]
            b = got_ref[pl.ds(pl.multiple_of((base + j) * 2, 2), 2), :]
            pair[pl.ds(pl.multiple_of((base + j) * 2, 2), 2), :] = a * b
        return carry

    lax.fori_loop(0, block // 32, some_edges, 0)
    total = None
    for half in range(2):
        value = pair[pl.ds(half, block, stride=2), :].astype(BF)
        part = lax.dot_general(
            map_ref[:, half * 128 : half * 128 + 128],
            value,
            (((1,), (1,)), ((), ())),
            preferred_element_type=F32,
        )
        total = part if total is None else total + part
    at = step * block + lax.broadcasted_iota(jnp.int32, (1, block), 1)
    out_ref[...] = jnp.where(at < count_ref[0], total, 0.0).astype(BF)


def edges_call(src, count, left, lower, upper, got, mapping):
    edges = src.shape[0]
    orb = mapping.shape[0]
    ghosts = lower.shape[0]
    whole = lambda a: pl.BlockSpec(a.shape, lambda i, *_: (0, 0))
    return pl.pallas_call(
        edges_kernel,
        out_shape=jax.ShapeDtypeStruct((orb, edges), BF),
        grid_spec=pltpu.PrefetchScalarGridSpec(
            num_scalar_prefetch=2,
            grid=(edges // TILE,),
            in_specs=[
                whole(left),
                whole(lower),
                whole(upper),
                pl.BlockSpec((2 * TILE, 128), lambda i, *_: (i, 0)),
                whole(mapping),
            ],
            out_specs=pl.BlockSpec((orb, TILE), lambda i, *_: (0, i)),
            scratch_shapes=[
                pltpu.VMEM((left.shape[0] + 4 * ghosts, 128), F32),
                pltpu.VMEM((2 * TILE, 128), F32),
            ],
        ),
        compiler_params=params(24),
        cost_estimate=pl.CostEstimate(flops=2 * edges * 256 * orb, transcendentals=0, bytes_accessed=8 << 20),
        name="edges",
    )(src, count, left, lower, upper, got, mapping)


def exchange(pieces, axes):
    return lax.all_to_all(pieces, axes, 0, 0, tiled=True)


def shift(value, axis, by):
    count = lax.axis_size(axis)
    return lax.ppermute(value, axis, [(i, (i + by) % count) for i in range(count)])


def local(
    particle_traits,
    particle_coordinates,
    kspace_vectors,
    learned_kspace_filter,
    spatial_home,
    following_halo_lines,
    previous_halo_lines,
    sender_projection,
    receiver_projection,
    pair_channel_mapping,
    vertex_rescaling_gain,
    link_sender_line,
    link_receiver_particle,
    active_link_tally,
):
    n_atoms = lax.axis_size(ATOM_AXES)
    n_planes = lax.axis_size(PLANE_AXES)
    n_x = lax.axis_size("x")
    n_kvec = lax.axis_size(KV_AXES)
    core = lax.axis_index("core")
    x, yl = lax.axis_index("x"), lax.axis_index("yl")
    atoms, chans = particle_traits.shape
    kdev = kspace_vectors.shape[1]
    norm_scale = 1.0 / math.sqrt(atoms * n_atoms * kdev * n_kvec)
    share = atoms // n_kvec
    run = atoms // n_atoms // n_kvec
    piece = kdev // n_atoms
    core_word = core.astype(jnp.int32)[None]

    keep, send = struct_call(core_word, particle_coordinates, kspace_vectors, particle_traits, n_planes)
    chip = (keep.astype(F32) + shift(send, "core", 1).astype(F32)).astype(BF)
    spread = exchange(chip, PLANE_AXES)

    home = spatial_home[0]
    goal = home // run % n_kvec
    tile = (1 - (goal // n_x + yl) % 2) * n_x + (goal - x + 2) % n_x
    own_tile = n_x + 2
    places = tile * share + home // (run * n_kvec) * run + home % run
    want = (places - own_tile * share)[None, :]
    ordered, krhs, feats = order_call(
        places, want, core_word, particle_coordinates, kspace_vectors, particle_traits, share
    )

    struct = jnp.sum(spread.astype(F32), axis=0)
    at = (core * n_planes + lax.axis_index(PLANE_AXES)) * piece
    filter_piece = lax.dynamic_slice_in_dim(learned_kspace_filter, at, piece, 0)
    filtered = (filter_piece[None] * struct * norm_scale).astype(BF)
    own = exchange(jnp.broadcast_to(filtered[None], (n_planes,) + filtered.shape), PLANE_AXES)
    other = shift(own, "core", 1)

    parts = []
    for j in (0, 1, 3, 2, 4, 5, 7, own_tile):
        value = update_call(j, ordered, krhs, own, other)
        if j != own_tile:
            dy, dx = 1 - j // n_x, (j % n_x + 2) % n_x
            pairs = [
                (a * n_x + b, (a + dy) % 2 * n_x + (b + dx) % n_x) for a in range(2) for b in range(n_x)
            ]
            value = lax.ppermute(value, KV_AXES, pairs)
        parts.append(value)
    node = node_call(parts, feats, vertex_rescaling_gain[None, :])
    mine = exchange(node.reshape(n_atoms, run, chans), ATOM_AXES)

    half = n_atoms // 2
    across = shift(mine, "yl", 1)
    before = shift(mine, "x", 1)
    after = shift(mine, "x", -1)
    far = (shift(before[:half], "x", 1), shift(after[half:], "x", -1))
    across_before = shift(across, "x", 1)
    across_after = shift(after, "yl", 1)
    across_far = tuple(shift(a, "yl", 1) for a in far)
    pieces = ((mine,), (after,), far, (before,), (across,), (across_after,), across_far, (across_before,))
    offsets = jnp.arange(n_kvec, dtype=jnp.int32)
    kvs = (yl + offsets // n_x) % 2 * n_x + (x + offsets % n_x) % n_x

    ids = jnp.concatenate([following_halo_lines[0], previous_halo_lines[0]]) * 2
    left, for_next, for_previous = halo_call(pieces, kvs, ids, sender_projection)
    lower = shift(for_next, ATOM_AXES, 1)
    upper = shift(for_previous, ATOM_AXES, -1)
    partition_rows, got = right_call(pieces, kvs, link_receiver_particle * 2, receiver_projection)
    orbital_blocks = edges_call(
        link_sender_line * 2, active_link_tally, left, lower, upper, got, pair_channel_mapping
    )
    return (orbital_blocks, partition_rows.reshape(atoms, chans))


def solution(mesh):
    fine = Mesh(mesh.devices.reshape(8, 2, 2, 2, 4), ATOM_AXES + KV_AXES)
    every = ATOM_AXES + KV_AXES
    placed = (
        P(ATOM_AXES, None),
        P(None, ATOM_AXES),
        P(None, KV_AXES),
        P(KV_AXES, None),
        P(ATOM_AXES, None),
        P(ATOM_AXES, None),
        P(ATOM_AXES, None),
        P(),
        P(),
        P(),
        P(),
        P(every),
        P(every),
        P(every),
    )
    return jax.shard_map(
        local,
        mesh=fine,
        in_specs=placed,
        out_specs=(P(None, every), P(ATOM_AXES, None)),
        check_vma=False,
    )
```

```python
import functools
import math

import jax
import jax.numpy as jnp
from jax import lax
from jax.experimental import pallas as pl
from jax.experimental.pallas import tpu as pltpu
from jax.sharding import Mesh
from jax.sharding import PartitionSpec as P


BF = jnp.bfloat16
F32 = jnp.float32
ATOM_AXES = ("z", "yh", "core")
PLANE_AXES = ("z", "yh")
KV_AXES = ("yl", "x")
TILE = 512
TRIG_ROWS = 16

SIN_TERMS = (
    4.442882919124345,
    -7.30824568650903,
    3.6063542184324517,
    -0.8461116503720991,
    0.10982451642340209,
)
COS_TERMS = (
    1.4142134962552282,
    -6.978850948563795,
    5.739460376906981,
    -1.8835579059858576,
    0.31068802752541236,
)


def cos_sin_of_turns(turns):
    r = turns - jnp.round(turns)
    z = r * r
    u = SIN_TERMS[4] * z + SIN_TERMS[3]
    v = COS_TERMS[4] * z + COS_TERMS[3]
    for term in (2, 1, 0):
        u = u * z + SIN_TERMS[term]
        v = v * z + COS_TERMS[term]
    u = u * r
    return 1.0 - u * u, u * v


def three_parts(values):
    first = values.astype(BF).astype(F32)
    rest = values - first
    second = rest.astype(BF).astype(F32)
    third = (rest - second).astype(BF).astype(F32)
    return first, second, third


def store_atom_parts(parts_ref, coordinates):
    a, b, c = three_parts(coordinates)
    for place, part in enumerate((a, a, a, b, b, c)):
        parts_ref[3 * place : 3 * place + 3, :] = part


def store_kspace_parts(parts_ref, vectors):
    a, b, c = three_parts(vectors * (0.5 / math.pi))
    for place, part in enumerate((a, b, c, a, b, a)):
        parts_ref[3 * place : 3 * place + 3, :] = part


def own_first(vectors, core):
    half = vectors.shape[1] // 2
    a, b = vectors[:, :half], vectors[:, half:]
    first = core == 0
    return jnp.concatenate([jnp.where(first, a, b), jnp.where(first, b, a)], axis=1)


def params(megabytes):
    return pltpu.CompilerParams(vmem_limit_bytes=megabytes << 20)


def struct_kernel(core_ref, coord_ref, kvec_ref, feat_ref, keep_ref, send_ref, apart, kpart, klhs, phase, cosv, sinv, acc):
    step = pl.program_id(0)
    kdev = kvec_ref.shape[1]

    @pl.when(step == 0)
    def _():
        apart[...] = jnp.zeros_like(apart)
        kpart[...] = jnp.zeros_like(kpart)
        store_kspace_parts(kpart, own_first(kvec_ref[...], core_ref[0]))
        klhs[...] = kpart[...].T.astype(BF)
        acc[...] = jnp.zeros_like(acc)

    store_atom_parts(apart, coord_ref[...])
    phase[...] = jnp.dot(klhs[...], apart[...].astype(BF), preferred_element_type=F32)

    def some_rows(i, carry):
        rows = pl.ds(pl.multiple_of(i * TRIG_ROWS, TRIG_ROWS), TRIG_ROWS)
        c, s = cos_sin_of_turns(phase[rows, :])
        cosv[rows, :] = c.astype(BF)
        sinv[rows, :] = s.astype(BF)
        return carry

    lax.fori_loop(0, kdev // TRIG_ROWS, some_rows, 0, unroll=4)
    acc[0] += jnp.dot(cosv[...], feat_ref[...], preferred_element_type=F32)
    acc[1] += jnp.dot(sinv[...], feat_ref[...], preferred_element_type=F32)

    @pl.when(step == pl.num_programs(0) - 1)
    def _():
        planes, _, piece, chans = keep_ref.shape
        half = kdev // 2
        for part in range(2):
            keep_ref[:, part] = acc[part, :half].reshape(planes, piece, chans).astype(BF)
            send_ref[:, part] = acc[part, half:].reshape(planes, piece, chans).astype(BF)


def struct_call(core, coordinates, vectors, feats, planes):
    atoms, chans = feats.shape
    kdev = vectors.shape[1]
    shape = (planes, 2, kdev // 2 // planes, chans)
    return pl.pallas_call(
        struct_kernel,
        out_shape=[jax.ShapeDtypeStruct(shape, BF)] * 2,
        grid_spec=pltpu.PrefetchScalarGridSpec(
            num_scalar_prefetch=1,
            grid=(atoms // TILE,),
            in_specs=[
                pl.BlockSpec((3, TILE), lambda i, c: (0, i)),
                pl.BlockSpec((3, kdev), lambda i, c: (0, 0)),
                pl.BlockSpec((TILE, chans), lambda i, c: (i, 0)),
            ],
            out_specs=[pl.BlockSpec(shape, lambda i, c: (0, 0, 0, 0))] * 2,
            scratch_shapes=[
                pltpu.VMEM((128, TILE), F32),
                pltpu.VMEM((128, kdev), F32),
                pltpu.VMEM((kdev, 128), BF),
                pltpu.VMEM((kdev, TILE), F32),
                pltpu.VMEM((kdev, TILE), BF),
                pltpu.VMEM((kdev, TILE), BF),
                pltpu.VMEM((2, kdev, chans), F32),
            ],
        ),
        compiler_params=params(16),
        cost_estimate=pl.CostEstimate(flops=6 * atoms * kdev * chans, transcendentals=0, bytes_accessed=4 << 20),
        name="struct",
    )(core, coordinates, vectors, feats)


def order_kernel(place_ref, core_ref, coord_ref, kvec_ref, ordered_ref, krhs_ref, apart, kpart, rows, ordered):
    atoms = coord_ref.shape[1]
    apart[...] = jnp.zeros_like(apart)
    kpart[...] = jnp.zeros_like(kpart)
    store_kspace_parts(kpart, own_first(kvec_ref[...], core_ref[0]))
    krhs_ref[...] = kpart[...].astype(BF)
    for part in range(atoms // TILE):
        span = slice(part * TILE, (part + 1) * TILE)
        store_atom_parts(apart, coord_ref[:, span])
        rows[span, :] = apart[...].T

    def move(i, carry):
        base = i * 32
        for j in range(32):
            ordered[pl.ds(place_ref[base + j], 1), :] = rows[pl.ds(base + j, 1), :]
        return carry

    lax.fori_loop(0, atoms // 32, move, 0)

    def narrow(i, carry):
        span = pl.ds(pl.multiple_of(i * TILE, TILE), TILE)
        ordered_ref[span, :] = ordered[span, :].astype(BF)
        return carry

    lax.fori_loop(0, atoms // TILE, narrow, 0)


def order_call(places, core, coordinates, vectors):
    atoms = coordinates.shape[1]
    kdev = vectors.shape[1]
    whole = pl.BlockSpec(memory_space=pltpu.VMEM)
    return pl.pallas_call(
        order_kernel,
        out_shape=(
            jax.ShapeDtypeStruct((atoms, 128), BF),
            jax.ShapeDtypeStruct((128, kdev), BF),
        ),
        grid_spec=pltpu.PrefetchScalarGridSpec(
            num_scalar_prefetch=2,
            grid=(),
            in_specs=[whole] * 2,
            out_specs=(whole,) * 2,
            scratch_shapes=[
                pltpu.VMEM((128, TILE), F32),
                pltpu.VMEM((128, kdev), F32),
                pltpu.VMEM((atoms, 128), F32),
                pltpu.VMEM((atoms, 128), F32),
            ],
        ),
        compiler_params=params(16),
        cost_estimate=pl.CostEstimate(flops=atoms * kdev * 1024, transcendentals=0, bytes_accessed=4 << 20),
        name="order",
    )(places, core, coordinates, vectors)


def pick_kernel(want_ref, feat_ref, picked_ref, acc):
    wanted = picked_ref.shape[0]
    hot = lax.broadcasted_iota(jnp.int32, (wanted, TILE), 0) == want_ref[...]
    got = jnp.dot(jnp.where(hot, 1.0, 0.0).astype(BF), feat_ref[...], preferred_element_type=F32)
    step = pl.program_id(0)

    @pl.when(step == 0)
    def _():
        acc[...] = got

    @pl.when(step > 0)
    def _():
        acc[...] += got

    @pl.when(step == pl.num_programs(0) - 1)
    def _():
        picked_ref[...] = acc[...].astype(BF)


def pick_call(want, feats, wanted):
    atoms, chans = feats.shape
    return pl.pallas_call(
        pick_kernel,
        out_shape=jax.ShapeDtypeStruct((wanted, chans), BF),
        grid=(atoms // TILE,),
        in_specs=[
            pl.BlockSpec((1, TILE), lambda i: (0, i)),
            pl.BlockSpec((TILE, chans), lambda i: (i, 0)),
        ],
        out_specs=pl.BlockSpec((wanted, chans), lambda i: (0, 0)),
        scratch_shapes=[pltpu.VMEM((wanted, chans), F32)],
        compiler_params=params(8),
        cost_estimate=pl.CostEstimate(flops=2 * atoms * wanted * chans, transcendentals=0, bytes_accessed=3 << 20),
        name="pick",
    )(want, feats)


def update_kernel(rows_ref, krhs_ref, own_ref, other_ref, out_ref, phase, cosv, sinv):
    kdev = krhs_ref.shape[1]
    half = kdev // 2
    phase[...] = jnp.dot(rows_ref[...], krhs_ref[...], preferred_element_type=F32)

    def some_rows(i, carry):
        span = pl.ds(pl.multiple_of(i * TRIG_ROWS, TRIG_ROWS), TRIG_ROWS)
        c, s = cos_sin_of_turns(phase[span, :])
        cosv[span, :] = c.astype(BF)
        sinv[span, :] = s.astype(BF)
        return carry

    lax.fori_loop(0, rows_ref.shape[0] // TRIG_ROWS, some_rows, 0, unroll=4)
    total = None
    for part, wave in enumerate((cosv, sinv)):
        for place, ref in enumerate((own_ref, other_ref)):
            weights = ref[:, part].reshape(half, -1)
            got = jnp.dot(wave[:, place * half : (place + 1) * half], weights, preferred_element_type=F32)
            total = got if total is None else total + got
    out_ref[...] = total.astype(BF)


def update_call(tile, ordered, krhs, own, other):
    kdev = krhs.shape[1]
    chans = own.shape[-1]
    whole = lambda a: pl.BlockSpec(a.shape, lambda i: (0,) * a.ndim)
    return pl.pallas_call(
        update_kernel,
        out_shape=jax.ShapeDtypeStruct((TILE, chans), BF),
        grid=(1,),
        in_specs=[pl.BlockSpec((TILE, 128), lambda i: (tile, 0)), whole(krhs), whole(own), whole(other)],
        out_specs=pl.BlockSpec((TILE, chans), lambda i: (0, 0)),
        scratch_shapes=[
            pltpu.VMEM((TILE, kdev), F32),
            pltpu.VMEM((TILE, kdev), BF),
            pltpu.VMEM((TILE, kdev), BF),
        ],
        compiler_params=params(12),
        cost_estimate=pl.CostEstimate(flops=4 * TILE * kdev * chans, transcendentals=0, bytes_accessed=1 << 20),
        name="update",
    )(ordered, krhs, own, other)


def merge_kernel(starts, cuts, *refs):
    base_ref, add_refs, out_refs = refs[0], refs[1 : 1 + len(starts)], refs[1 + len(starts) :]
    at = 0
    for cut, out_ref in zip(cuts, out_refs):
        edges = {at, at + cut}
        for start, ref in zip(starts, add_refs):
            edges |= {e for e in (start, start + ref.shape[0]) if at < e < at + cut}
        edges = sorted(edges)
        for low, high in zip(edges[:-1], edges[1:]):
            value = base_ref[low:high, :].astype(F32)
            for start, ref in zip(starts, add_refs):
                if start <= low and high <= start + ref.shape[0]:
                    value = value + ref[low - start : high - start, :].astype(F32)
            out_ref[low - at : high - at, :] = value.astype(BF)
        at += cut


def merge_call(base, addends, cuts):
    arrays = [base] + [a for a, _ in addends]
    whole = pl.BlockSpec(memory_space=pltpu.VMEM)
    return pl.pallas_call(
        functools.partial(merge_kernel, tuple(s for _, s in addends), cuts),
        out_shape=[jax.ShapeDtypeStruct((cut, base.shape[1]), BF) for cut in cuts],
        in_specs=[whole] * len(arrays),
        out_specs=[whole] * len(cuts),
        compiler_params=params(4),
        cost_estimate=pl.CostEstimate(flops=base.size, transcendentals=0, bytes_accessed=1 << 20),
        name="merge",
    )(*arrays)


def node_kernel(*refs):
    *part_refs, feat_ref, gain_ref, out_ref = refs
    update = part_refs[0][...].astype(F32)
    for ref in part_refs[1:]:
        update = update + ref[...].astype(F32)
    refreshed = feat_ref[...].astype(F32) + update / (1.0 + jnp.exp(-update))
    mean = jnp.mean(refreshed * refreshed, axis=-1, keepdims=True)
    out_ref[...] = (refreshed * lax.rsqrt(mean + 1e-06) * gain_ref[...]).astype(BF)


def node_call(parts, feats, gain):
    rows, chans = feats.shape
    block = 256
    tile = pl.BlockSpec((block, chans), lambda i: (i, 0))
    return pl.pallas_call(
        node_kernel,
        out_shape=jax.ShapeDtypeStruct((rows, chans), BF),
        grid=(rows // block,),
        in_specs=[tile] * (len(parts) + 1) + [pl.BlockSpec((1, chans), lambda i: (0, 0))],
        out_specs=tile,
        compiler_params=params(8),
        cost_estimate=pl.CostEstimate(flops=20 * rows * chans, transcendentals=rows * chans, bytes_accessed=3 << 20),
        name="node",
    )(*parts, feats, gain)


def pairs_of(piece_refs):
    for kv, refs in enumerate(piece_refs):
        at = 0
        for ref in refs:
            yield kv, at, ref
            at += ref.shape[0]


def store_rows(table, value, starts, run):
    for place, start in enumerate(starts):
        for half in range(2):
            table[pl.ds(start + half, run, stride=2), :] = value[
                place * run : (place + 1) * run, half * 128 : half * 128 + 128
            ]


def project_pieces(piece_refs, kv_ref, weight_ref, table, spots):
    for kv, at, ref in pairs_of(piece_refs):
        count, run, chans = ref.shape
        rows = ref[...].reshape(count * run, chans)
        got = jnp.dot(rows, weight_ref[...], preferred_element_type=F32).astype(BF).astype(F32)
        base = pl.multiple_of(kv_ref[kv] * (2 * run), 2 * run)
        starts = [base + (at + s) * (2 * run * spots) for s in range(count)]
        store_rows(table, got, starts, run)


def halo_kernel(split, kv_ref, ids_ref, *refs):
    flat, (weight_ref, left_ref, down_ref, up_ref, picked) = refs[: sum(split)], refs[sum(split) :]
    pieces, at = [], 0
    for count in split:
        pieces.append(flat[at : at + count])
        at += count
    project_pieces(pieces, kv_ref, weight_ref, left_ref, len(split))
    halo = ids_ref.shape[0]

    def move(i, carry):
        base = i * 32
        for j in range(32):
            row = left_ref[pl.ds(pl.multiple_of(ids_ref[base + j], 2), 2), :]
            picked[pl.ds(pl.multiple_of((base + j) * 2, 2), 2), :] = row
        return carry

    lax.fori_loop(0, halo // 32, move, 0)
    for side, ref in enumerate((down_ref, up_ref)):
        for half in range(2):
            rows = picked[pl.ds(side * halo + half, halo // 2, stride=2), :]
            ref[:, half * 128 : half * 128 + 128] = rows.astype(BF)


def halo_call(pieces, kvs, ids, weight):
    split = tuple(len(p) for p in pieces)
    flat = [a for p in pieces for a in p]
    chans = weight.shape[0]
    halo = ids.shape[0]
    rows = sum(a.shape[0] * a.shape[1] for a in flat)
    whole = pl.BlockSpec(memory_space=pltpu.VMEM)
    return pl.pallas_call(
        functools.partial(halo_kernel, split),
        out_shape=(
            jax.ShapeDtypeStruct((2 * rows, 128), F32),
            jax.ShapeDtypeStruct((halo // 2, chans), BF),
            jax.ShapeDtypeStruct((halo // 2, chans), BF),
        ),
        grid_spec=pltpu.PrefetchScalarGridSpec(
            num_scalar_prefetch=2,
            grid=(),
            in_specs=[whole] * (len(flat) + 1),
            out_specs=(whole,) * 3,
            scratch_shapes=[pltpu.VMEM((2 * halo, 128), F32)],
        ),
        compiler_params=params(16),
        cost_estimate=pl.CostEstimate(flops=2 * rows * chans * chans, transcendentals=0, bytes_accessed=8 << 20),
        name="halo",
    )(kvs, ids, *flat, weight)


def right_kernel(split, kv_ref, dst_ref, *refs):
    flat, (weight_ref, out_ref, got_ref, table) = refs[: sum(split)], refs[sum(split) :]
    pieces, at = [], 0
    for count in split:
        pieces.append(flat[at : at + count])
        at += count
    for kv, at, ref in pairs_of(pieces):
        out_ref[at : at + ref.shape[0], kv_ref[kv]] = ref[...]
    project_pieces(pieces, kv_ref, weight_ref, table, len(split))

    def move(i, carry):
        base = i * 32
        for j in range(32):
            row = table[pl.ds(pl.multiple_of(dst_ref[base + j], 2), 2), :]
            got_ref[pl.ds(pl.multiple_of((base + j) * 2, 2), 2), :] = row
        return carry

    lax.fori_loop(0, dst_ref.shape[0] // 32, move, 0)


def right_call(pieces, kvs, dst, weight):
    split = tuple(len(p) for p in pieces)
    flat = [a for p in pieces for a in p]
    count, run, chans = pieces[0][0].shape
    edges = dst.shape[0]
    rows = sum(a.shape[0] * a.shape[1] for a in flat)
    whole = pl.BlockSpec(memory_space=pltpu.VMEM)
    return pl.pallas_call(
        functools.partial(right_kernel, split),
        out_shape=(
            jax.ShapeDtypeStruct((count, len(split), run, chans), BF),
            jax.ShapeDtypeStruct((2 * edges, 128), F32),
        ),
        grid_spec=pltpu.PrefetchScalarGridSpec(
            num_scalar_prefetch=2,
            grid=(),
            in_specs=[whole] * (len(flat) + 1),
            out_specs=(whole,) * 2,
            scratch_shapes=[pltpu.VMEM((2 * rows, 128), F32)],
        ),
        compiler_params=params(20),
        cost_estimate=pl.CostEstimate(flops=2 * rows * chans * chans, transcendentals=0, bytes_accessed=8 << 20),
        name="right",
    )(kvs, dst, *flat, weight)


def edges_kernel(src_ref, count_ref, left_ref, lower_ref, upper_ref, got_ref, map_ref, out_ref, table, pair):
    step = pl.program_id(0)
    own = left_ref.shape[0]
    ghosts = lower_ref.shape[0]
    block = out_ref.shape[1]

    @pl.when(step == 0)
    def _():
        table[:own, :] = left_ref[...]
        for side, ref in enumerate((lower_ref, upper_ref)):
            value = ref[...].astype(F32)
            store_rows(table, value, [own + side * 2 * ghosts], ghosts)

    def some_edges(i, carry):
        base = i * 32
        for j in range(32):
            at = step * block + base + j
            a = table[pl.ds(pl.multiple_of(src_ref[at], 2), 2), :]
            b = got_ref[pl.ds(pl.multiple_of((base + j) * 2, 2), 2), :]
            pair[pl.ds(pl.multiple_of((base + j) * 2, 2), 2), :] = a * b
        return carry

    lax.fori_loop(0, block // 32, some_edges, 0)
    total = None
    for half in range(2):
        value = pair[pl.ds(half, block, stride=2), :].astype(BF)
        part = lax.dot_general(
            map_ref[:, half * 128 : half * 128 + 128],
            value,
            (((1,), (1,)), ((), ())),
            preferred_element_type=F32,
        )
        total = part if total is None else total + part
    at = step * block + lax.broadcasted_iota(jnp.int32, (1, block), 1)
    out_ref[...] = jnp.where(at < count_ref[0], total, 0.0).astype(BF)


def edges_call(src, count, left, lower, upper, got, mapping):
    edges = src.shape[0]
    orb = mapping.shape[0]
    ghosts = lower.shape[0]
    whole = lambda a: pl.BlockSpec(a.shape, lambda i, *_: (0, 0))
    return pl.pallas_call(
        edges_kernel,
        out_shape=jax.ShapeDtypeStruct((orb, edges), BF),
        grid_spec=pltpu.PrefetchScalarGridSpec(
            num_scalar_prefetch=2,
            grid=(edges // TILE,),
            in_specs=[
                whole(left),
                whole(lower),
                whole(upper),
                pl.BlockSpec((2 * TILE, 128), lambda i, *_: (i, 0)),
                whole(mapping),
            ],
            out_specs=pl.BlockSpec((orb, TILE), lambda i, *_: (0, i)),
            scratch_shapes=[
                pltpu.VMEM((left.shape[0] + 4 * ghosts, 128), F32),
                pltpu.VMEM((2 * TILE, 128), F32),
            ],
        ),
        compiler_params=params(24),
        cost_estimate=pl.CostEstimate(flops=2 * edges * 256 * orb, transcendentals=0, bytes_accessed=8 << 20),
        name="edges",
    )(src, count, left, lower, upper, got, mapping)


def exchange(pieces, axes):
    return lax.all_to_all(pieces, axes, 0, 0, tiled=True)


def shift(value, axis, by):
    count = lax.axis_size(axis)
    return lax.ppermute(value, axis, [(i, (i + by) % count) for i in range(count)])


def local(
    particle_traits,
    particle_coordinates,
    kspace_vectors,
    learned_kspace_filter,
    spatial_home,
    following_halo_lines,
    previous_halo_lines,
    sender_projection,
    receiver_projection,
    pair_channel_mapping,
    vertex_rescaling_gain,
    link_sender_line,
    link_receiver_particle,
    active_link_tally,
):
    n_atoms = lax.axis_size(ATOM_AXES)
    n_planes = lax.axis_size(PLANE_AXES)
    n_x = lax.axis_size("x")
    n_kvec = lax.axis_size(KV_AXES)
    core = lax.axis_index("core")
    x, yl = lax.axis_index("x"), lax.axis_index("yl")
    atoms, chans = particle_traits.shape
    kdev = kspace_vectors.shape[1]
    norm_scale = 1.0 / math.sqrt(atoms * n_atoms * kdev * n_kvec)
    share = atoms // n_kvec
    run = atoms // n_atoms // n_kvec
    piece = kdev // n_atoms
    core_word = core.astype(jnp.int32)[None]

    in_hbm = lambda a: pltpu.with_memory_space_constraint(a, pltpu.HBM)
    keep, send = struct_call(
        core_word,
        in_hbm(particle_coordinates),
        in_hbm(kspace_vectors),
        in_hbm(particle_traits),
        n_planes,
    )
    chip = (keep.astype(F32) + shift(send, "core", 1).astype(F32)).astype(BF)
    spread = exchange(chip, PLANE_AXES)

    home = spatial_home[0]
    goal = home // run % n_kvec
    tile = (1 - (goal // n_x + yl) % 2) * n_x + (goal - x + 2) % n_x
    own_tile = n_x + 2
    places = tile * share + home // (run * n_kvec) * run + home % run
    want = (places - own_tile * share)[None, :]
    ordered, krhs = order_call(places, core_word, particle_coordinates, kspace_vectors)
    feats = pick_call(want, in_hbm(particle_traits), share)

    struct = jnp.sum(spread.astype(F32), axis=0)
    at = (core * n_planes + lax.axis_index(PLANE_AXES)) * piece
    filter_piece = lax.dynamic_slice_in_dim(learned_kspace_filter, at, piece, 0)
    filtered = (filter_piece[None] * struct * norm_scale).astype(BF)
    own = exchange(jnp.broadcast_to(filtered[None], (n_planes,) + filtered.shape), PLANE_AXES)
    other = shift(own, "core", 1)

    def towards(dy, dx):
        return update_call((1 - dy) * n_x + (dx + 2) % n_x, ordered, krhs, own, other)

    middle = share // 2
    far_across = shift(towards(1, 2), "yl", 1)
    before_across = shift(towards(1, -1), "yl", 1)
    after_across = shift(towards(1, 1), "x", 1)
    far_first, far_second = merge_call(
        towards(0, 2), ((far_across, 0),), (middle, share - middle)
    )
    far_first = shift(far_first, "x", 1)
    far_second = shift(far_second, "x", -1)
    (whole_across,) = merge_call(towards(1, 0), ((after_across, 0),), (share,))
    whole_across = shift(whole_across, "yl", 1)
    (whole_after,) = merge_call(towards(0, 1), ((far_first, 0),), (share,))
    whole_after = shift(whole_after, "x", 1)
    (whole_before,) = merge_call(
        towards(0, -1), ((before_across, 0), (far_second, middle)), (share,)
    )
    whole_before = shift(whole_before, "x", -1)
    parts = [towards(0, 0), whole_across, whole_after, whole_before]
    node = node_call(parts, feats, vertex_rescaling_gain[None, :])
    mine = exchange(node.reshape(n_atoms, run, chans), ATOM_AXES)

    half = n_atoms // 2
    across = shift(mine, "yl", 1)
    before = shift(mine, "x", 1)
    after = shift(mine, "x", -1)
    far = (shift(before[:half], "x", 1), shift(after[half:], "x", -1))
    across_before = shift(across, "x", 1)
    across_after = shift(after, "yl", 1)
    across_far = tuple(shift(a, "yl", 1) for a in far)
    pieces = ((mine,), (after,), far, (before,), (across,), (across_after,), across_far, (across_before,))
    offsets = jnp.arange(n_kvec, dtype=jnp.int32)
    kvs = (yl + offsets // n_x) % 2 * n_x + (x + offsets % n_x) % n_x

    ids = jnp.concatenate([following_halo_lines[0], previous_halo_lines[0]]) * 2
    left, for_next, for_previous = halo_call(pieces, kvs, ids, sender_projection)
    lower = shift(for_next, ATOM_AXES, 1)
    upper = shift(for_previous, ATOM_AXES, -1)
    partition_rows, got = right_call(pieces, kvs, link_receiver_particle * 2, receiver_projection)
    orbital_blocks = edges_call(
        link_sender_line * 2, active_link_tally, left, lower, upper, got, pair_channel_mapping
    )
    return (orbital_blocks, partition_rows.reshape(atoms, chans))


def solution(mesh):
    fine = Mesh(mesh.devices.reshape(8, 2, 2, 2, 4), ATOM_AXES + KV_AXES)
    every = ATOM_AXES + KV_AXES
    placed = (
        P(ATOM_AXES, None),
        P(None, ATOM_AXES),
        P(None, KV_AXES),
        P(KV_AXES, None),
        P(ATOM_AXES, None),
        P(ATOM_AXES, None),
        P(ATOM_AXES, None),
        P(),
        P(),
        P(),
        P(),
        P(every),
        P(every),
        P(every),
    )
    return jax.shard_map(
        local,
        mesh=fine,
        in_specs=placed,
        out_specs=(P(None, every), P(ATOM_AXES, None)),
        check_vma=False,
    )
```

```python
import functools
import math

import jax
import jax.numpy as jnp
from jax import lax
from jax.experimental import pallas as pl
from jax.experimental.pallas import tpu as pltpu
from jax.sharding import Mesh
from jax.sharding import PartitionSpec as P


BF = jnp.bfloat16
F32 = jnp.float32
ATOM_AXES = ("z", "yh", "core")
PLANE_AXES = ("z", "yh")
KV_AXES = ("yl", "x")
TILE = 512
TRIG_ROWS = 16
EDGE_BLOCK = 256

SIN_TERMS = (
    4.442882919124345,
    -7.30824568650903,
    3.6063542184324517,
    -0.8461116503720991,
    0.10982451642340209,
)
COS_TERMS = (
    1.4142134962552282,
    -6.978850948563795,
    5.739460376906981,
    -1.8835579059858576,
    0.31068802752541236,
)


def cos_sin_of_turns(turns):
    r = turns - jnp.round(turns)
    z = r * r
    u = SIN_TERMS[4] * z + SIN_TERMS[3]
    v = COS_TERMS[4] * z + COS_TERMS[3]
    for term in (2, 1, 0):
        u = u * z + SIN_TERMS[term]
        v = v * z + COS_TERMS[term]
    u = u * r
    return 1.0 - u * u, u * v


def three_parts(values):
    first = values.astype(BF).astype(F32)
    rest = values - first
    second = rest.astype(BF).astype(F32)
    third = (rest - second).astype(BF).astype(F32)
    return first, second, third


def store_atom_parts(parts_ref, coordinates):
    a, b, c = three_parts(coordinates)
    for place, part in enumerate((a, a, a, b, b, c)):
        parts_ref[3 * place : 3 * place + 3, :] = part


def store_kspace_parts(parts_ref, vectors):
    a, b, c = three_parts(vectors * (0.5 / math.pi))
    for place, part in enumerate((a, b, c, a, b, a)):
        parts_ref[3 * place : 3 * place + 3, :] = part


def own_first(vectors, core):
    half = vectors.shape[1] // 2
    a, b = vectors[:, :half], vectors[:, half:]
    first = core == 0
    return jnp.concatenate([jnp.where(first, a, b), jnp.where(first, b, a)], axis=1)


def params(megabytes):
    return pltpu.CompilerParams(vmem_limit_bytes=megabytes << 20)


def trig_rows(phase_ref, wave_ref, source, target, sine_target, count):
    for at in range(0, count, TRIG_ROWS):
        c, s = cos_sin_of_turns(phase_ref[pl.ds(source + at, TRIG_ROWS), :])
        wave_ref[pl.ds(target + at, TRIG_ROWS), :] = c.astype(BF)
        wave_ref[pl.ds(sine_target + at, TRIG_ROWS), :] = s.astype(BF)


def struct_kernel(core_ref, coord_ref, kvec_ref, feat_ref, keep_ref, send_ref, apart, kpart, klhs, phase_a, phase_b, wave_a, wave_b, feat_b, acc):
    step = pl.program_id(0)
    last = pl.num_programs(0) - 1
    kdev = kvec_ref.shape[1]
    block = 128

    def parts_of(tile):
        store_atom_parts(apart, coord_ref[:, pl.ds(pl.multiple_of(tile * TILE, TILE), TILE)])
        return apart[...].astype(BF)

    @pl.when(step == 0)
    def _():
        apart[...] = jnp.zeros_like(apart)
        kpart[...] = jnp.zeros_like(kpart)
        store_kspace_parts(kpart, own_first(kvec_ref[...], core_ref[0]))
        klhs[...] = kpart[...].T.astype(BF)
        acc[...] = jnp.zeros_like(acc)
        wave_b[...] = jnp.zeros_like(wave_b)
        feat_b[...] = jnp.zeros_like(feat_b)
        phase_a[...] = jnp.dot(klhs[...], parts_of(0), preferred_element_type=F32)

    def turn(next_tile, phase, next_phase, wave, done_wave, done_feat):
        parts = parts_of(next_tile)

        def some(c, carry):
            k = pl.multiple_of(c * block, block)
            w = pl.multiple_of(c * 2 * block, 2 * block)
            acc[pl.ds(w, 2 * block), :] += jnp.dot(
                done_wave[pl.ds(w, 2 * block), :], done_feat, preferred_element_type=F32
            )
            next_phase[pl.ds(k, block), :] = jnp.dot(
                klhs[pl.ds(k, block), :], parts, preferred_element_type=F32
            )
            trig_rows(phase, wave, k, w, w + block, block)
            return carry

        lax.fori_loop(0, kdev // block, some, 0)

    turn(2 * step + 1, phase_a, phase_b, wave_a, wave_b, feat_b[...])
    turn(jnp.minimum(2 * step + 2, 2 * last + 1), phase_b, phase_a, wave_b, wave_a, feat_ref[:TILE, :])
    feat_b[...] = feat_ref[TILE:, :]

    @pl.when(step == last)
    def _():
        acc[...] += jnp.dot(wave_b[...], feat_b[...], preferred_element_type=F32)
        _, _, piece, chans = keep_ref.shape
        blocks = kdev // block
        for c in range(blocks):
            ref = keep_ref if c < blocks // 2 else send_ref
            at = c % (blocks // 2) * (block // piece)
            for part in range(2):
                row = (2 * c + part) * block
                ref[at : at + block // piece, part] = (
                    acc[row : row + block, :].reshape(block // piece, piece, chans).astype(BF)
                )


def struct_call(core, coordinates, vectors, feats, planes):
    atoms, chans = feats.shape
    kdev = vectors.shape[1]
    shape = (planes, 2, kdev // 2 // planes, chans)
    return pl.pallas_call(
        struct_kernel,
        out_shape=[jax.ShapeDtypeStruct(shape, BF)] * 2,
        grid_spec=pltpu.PrefetchScalarGridSpec(
            num_scalar_prefetch=1,
            grid=(atoms // TILE // 2,),
            in_specs=[
                pl.BlockSpec((3, atoms), lambda i, c: (0, 0)),
                pl.BlockSpec((3, kdev), lambda i, c: (0, 0)),
                pl.BlockSpec((2 * TILE, chans), lambda i, c: (i, 0)),
            ],
            out_specs=[pl.BlockSpec(shape, lambda i, c: (0, 0, 0, 0))] * 2,
            scratch_shapes=[
                pltpu.VMEM((128, TILE), F32),
                pltpu.VMEM((128, kdev), F32),
                pltpu.VMEM((kdev, 128), BF),
                pltpu.VMEM((kdev, TILE), F32),
                pltpu.VMEM((kdev, TILE), F32),
                pltpu.VMEM((2 * kdev, TILE), BF),
                pltpu.VMEM((2 * kdev, TILE), BF),
                pltpu.VMEM((TILE, chans), BF),
                pltpu.VMEM((2 * kdev, chans), F32),
            ],
        ),
        compiler_params=params(16),
        cost_estimate=pl.CostEstimate(flops=6 * atoms * kdev * chans, transcendentals=0, bytes_accessed=4 << 20),
        name="struct",
    )(core, coordinates, vectors, feats)


def order_kernel(place_ref, core_ref, coord_ref, kvec_ref, ordered_ref, krhs_ref, apart, kpart, rows, ordered):
    atoms = coord_ref.shape[1]
    apart[...] = jnp.zeros_like(apart)
    kpart[...] = jnp.zeros_like(kpart)
    store_kspace_parts(kpart, own_first(kvec_ref[...], core_ref[0]))
    krhs_ref[...] = kpart[...].astype(BF)
    for part in range(atoms // TILE):
        span = slice(part * TILE, (part + 1) * TILE)
        store_atom_parts(apart, coord_ref[:, span])
        rows[span, :] = apart[...].T

    def move(i, carry):
        base = i * 32
        for j in range(32):
            ordered[pl.ds(place_ref[base + j], 1), :] = rows[pl.ds(base + j, 1), :]
        return carry

    lax.fori_loop(0, atoms // 32, move, 0)

    def narrow(i, carry):
        span = pl.ds(pl.multiple_of(i * TILE, TILE), TILE)
        ordered_ref[span, :] = ordered[span, :].astype(BF)
        return carry

    lax.fori_loop(0, atoms // TILE, narrow, 0)


def order_call(places, core, coordinates, vectors):
    atoms = coordinates.shape[1]
    kdev = vectors.shape[1]
    whole = pl.BlockSpec(memory_space=pltpu.VMEM)
    return pl.pallas_call(
        order_kernel,
        out_shape=(
            jax.ShapeDtypeStruct((atoms, 128), BF),
            jax.ShapeDtypeStruct((128, kdev), BF),
        ),
        grid_spec=pltpu.PrefetchScalarGridSpec(
            num_scalar_prefetch=2,
            grid=(),
            in_specs=[whole] * 2,
            out_specs=(whole,) * 2,
            scratch_shapes=[
                pltpu.VMEM((128, TILE), F32),
                pltpu.VMEM((128, kdev), F32),
                pltpu.VMEM((atoms, 128), F32),
                pltpu.VMEM((atoms, 128), F32),
            ],
        ),
        compiler_params=params(16),
        cost_estimate=pl.CostEstimate(flops=atoms * kdev * 1024, transcendentals=0, bytes_accessed=4 << 20),
        name="order",
    )(places, core, coordinates, vectors)


def pick_kernel(want_ref, feat_ref, picked_ref, acc):
    wanted = picked_ref.shape[0]
    hot = lax.broadcasted_iota(jnp.int32, (wanted, TILE), 0) == want_ref[...]
    got = jnp.dot(jnp.where(hot, 1.0, 0.0).astype(BF), feat_ref[...], preferred_element_type=F32)
    step = pl.program_id(0)

    @pl.when(step == 0)
    def _():
        acc[...] = got

    @pl.when(step > 0)
    def _():
        acc[...] += got

    @pl.when(step == pl.num_programs(0) - 1)
    def _():
        picked_ref[...] = acc[...].astype(BF)


def pick_call(want, feats, wanted):
    atoms, chans = feats.shape
    return pl.pallas_call(
        pick_kernel,
        out_shape=jax.ShapeDtypeStruct((wanted, chans), BF),
        grid=(atoms // TILE,),
        in_specs=[
            pl.BlockSpec((1, TILE), lambda i: (0, i)),
            pl.BlockSpec((TILE, chans), lambda i: (i, 0)),
        ],
        out_specs=pl.BlockSpec((wanted, chans), lambda i: (0, 0)),
        scratch_shapes=[pltpu.VMEM((wanted, chans), F32)],
        compiler_params=params(8),
        cost_estimate=pl.CostEstimate(flops=2 * atoms * wanted * chans, transcendentals=0, bytes_accessed=3 << 20),
        name="pick",
    )(want, feats)


def update_kernel(rows_ref, krhs_ref, own_ref, other_ref, out_ref, phase, cosv, sinv):
    kdev = krhs_ref.shape[1]
    half = kdev // 2
    phase[...] = jnp.dot(rows_ref[...], krhs_ref[...], preferred_element_type=F32)

    def some_rows(i, carry):
        span = pl.ds(pl.multiple_of(i * TRIG_ROWS, TRIG_ROWS), TRIG_ROWS)
        c, s = cos_sin_of_turns(phase[span, :])
        cosv[span, :] = c.astype(BF)
        sinv[span, :] = s.astype(BF)
        return carry

    lax.fori_loop(0, rows_ref.shape[0] // TRIG_ROWS, some_rows, 0, unroll=4)
    total = None
    for part, wave in enumerate((cosv, sinv)):
        for place, ref in enumerate((own_ref, other_ref)):
            weights = ref[:, part].reshape(half, -1)
            got = jnp.dot(wave[:, place * half : (place + 1) * half], weights, preferred_element_type=F32)
            total = got if total is None else total + got
    out_ref[...] = total.astype(BF)


def update_call(tile, ordered, krhs, own, other):
    kdev = krhs.shape[1]
    chans = own.shape[-1]
    whole = lambda a: pl.BlockSpec(a.shape, lambda i: (0,) * a.ndim)
    return pl.pallas_call(
        update_kernel,
        out_shape=jax.ShapeDtypeStruct((TILE, chans), BF),
        grid=(1,),
        in_specs=[pl.BlockSpec((TILE, 128), lambda i: (tile, 0)), whole(krhs), whole(own), whole(other)],
        out_specs=pl.BlockSpec((TILE, chans), lambda i: (0, 0)),
        scratch_shapes=[
            pltpu.VMEM((TILE, kdev), F32),
            pltpu.VMEM((TILE, kdev), BF),
            pltpu.VMEM((TILE, kdev), BF),
        ],
        compiler_params=params(12),
        cost_estimate=pl.CostEstimate(flops=4 * TILE * kdev * chans, transcendentals=0, bytes_accessed=1 << 20),
        name="update",
    )(ordered, krhs, own, other)


def merge_kernel(starts, cuts, *refs):
    base_ref, add_refs, out_refs = refs[0], refs[1 : 1 + len(starts)], refs[1 + len(starts) :]
    at = 0
    for cut, out_ref in zip(cuts, out_refs):
        edges = {at, at + cut}
        for start, ref in zip(starts, add_refs):
            edges |= {e for e in (start, start + ref.shape[0]) if at < e < at + cut}
        edges = sorted(edges)
        for low, high in zip(edges[:-1], edges[1:]):
            value = base_ref[low:high, :].astype(F32)
            for start, ref in zip(starts, add_refs):
                if start <= low and high <= start + ref.shape[0]:
                    value = value + ref[low - start : high - start, :].astype(F32)
            out_ref[low - at : high - at, :] = value.astype(BF)
        at += cut


def merge_call(base, addends, cuts):
    arrays = [base] + [a for a, _ in addends]
    whole = pl.BlockSpec(memory_space=pltpu.VMEM)
    return pl.pallas_call(
        functools.partial(merge_kernel, tuple(s for _, s in addends), cuts),
        out_shape=[jax.ShapeDtypeStruct((cut, base.shape[1]), BF) for cut in cuts],
        in_specs=[whole] * len(arrays),
        out_specs=[whole] * len(cuts),
        compiler_params=params(4),
        cost_estimate=pl.CostEstimate(flops=base.size, transcendentals=0, bytes_accessed=1 << 20),
        name="merge",
    )(*arrays)


def node_kernel(*refs):
    *part_refs, feat_ref, gain_ref, out_ref = refs
    update = part_refs[0][...].astype(F32)
    for ref in part_refs[1:]:
        update = update + ref[...].astype(F32)
    refreshed = feat_ref[...].astype(F32) + update / (1.0 + jnp.exp(-update))
    mean = jnp.mean(refreshed * refreshed, axis=-1, keepdims=True)
    out_ref[...] = (refreshed * lax.rsqrt(mean + 1e-06) * gain_ref[...]).astype(BF)


def node_call(parts, feats, gain):
    rows, chans = feats.shape
    block = 256
    tile = pl.BlockSpec((block, chans), lambda i: (i, 0))
    return pl.pallas_call(
        node_kernel,
        out_shape=jax.ShapeDtypeStruct((rows, chans), BF),
        grid=(rows // block,),
        in_specs=[tile] * (len(parts) + 1) + [pl.BlockSpec((1, chans), lambda i: (0, 0))],
        out_specs=tile,
        compiler_params=params(8),
        cost_estimate=pl.CostEstimate(flops=20 * rows * chans, transcendentals=rows * chans, bytes_accessed=3 << 20),
        name="node",
    )(*parts, feats, gain)


def pairs_of(piece_refs):
    for kv, refs in enumerate(piece_refs):
        at = 0
        for ref in refs:
            yield kv, at, ref
            at += ref.shape[0]


def store_rows(table, value, starts, run):
    for place, start in enumerate(starts):
        for half in range(2):
            table[pl.ds(start + half, run, stride=2), :] = value[
                place * run : (place + 1) * run, half * 128 : half * 128 + 128
            ]


def project_pieces(piece_refs, kv_ref, weight_ref, table, spots):
    for kv, at, ref in pairs_of(piece_refs):
        count, run, chans = ref.shape
        rows = ref[...].reshape(count * run, chans)
        got = jnp.dot(rows, weight_ref[...], preferred_element_type=F32).astype(BF).astype(F32)
        base = pl.multiple_of(kv_ref[kv] * (2 * run), 2 * run)
        starts = [base + (at + s) * (2 * run * spots) for s in range(count)]
        store_rows(table, got, starts, run)


def halo_kernel(split, kv_ref, ids_ref, *refs):
    flat, (weight_ref, left_ref, down_ref, up_ref, picked) = refs[: sum(split)], refs[sum(split) :]
    pieces, at = [], 0
    for count in split:
        pieces.append(flat[at : at + count])
        at += count
    project_pieces(pieces, kv_ref, weight_ref, left_ref, len(split))
    halo = ids_ref.shape[0]

    def move(i, carry):
        base = i * 32
        for j in range(32):
            row = left_ref[pl.ds(pl.multiple_of(ids_ref[base + j], 2), 2), :]
            picked[pl.ds(pl.multiple_of((base + j) * 2, 2), 2), :] = row
        return carry

    lax.fori_loop(0, halo // 32, move, 0)
    for side, ref in enumerate((down_ref, up_ref)):
        for half in range(2):
            rows = picked[pl.ds(side * halo + half, halo // 2, stride=2), :]
            ref[:, half * 128 : half * 128 + 128] = rows.astype(BF)


def halo_call(pieces, kvs, ids, weight):
    split = tuple(len(p) for p in pieces)
    flat = [a for p in pieces for a in p]
    chans = weight.shape[0]
    halo = ids.shape[0]
    rows = sum(a.shape[0] * a.shape[1] for a in flat)
    whole = pl.BlockSpec(memory_space=pltpu.VMEM)
    return pl.pallas_call(
        functools.partial(halo_kernel, split),
        out_shape=(
            jax.ShapeDtypeStruct((2 * (rows + halo), 128), F32),
            jax.ShapeDtypeStruct((halo // 2, chans), BF),
            jax.ShapeDtypeStruct((halo // 2, chans), BF),
        ),
        grid_spec=pltpu.PrefetchScalarGridSpec(
            num_scalar_prefetch=2,
            grid=(),
            in_specs=[whole] * (len(flat) + 1),
            out_specs=(whole,) * 3,
            scratch_shapes=[pltpu.VMEM((2 * halo, 128), F32)],
        ),
        compiler_params=params(16),
        cost_estimate=pl.CostEstimate(flops=2 * rows * chans * chans, transcendentals=0, bytes_accessed=8 << 20),
        name="halo",
    )(kvs, ids, *flat, weight)


def right_kernel(split, kv_ref, dst_ref, *refs):
    flat, (weight_ref, out_ref, got_ref, table, whole, sem) = refs[: sum(split)], refs[sum(split) :]
    pieces, at = [], 0
    for count in split:
        pieces.append(flat[at : at + count])
        at += count
    for kv, at, ref in pairs_of(pieces):
        whole[at : at + ref.shape[0], kv_ref[kv]] = ref[...]
    project_pieces(pieces, kv_ref, weight_ref, table, len(split))
    out = pltpu.make_async_copy(whole, out_ref, sem)
    out.start()

    def move(i, carry):
        base = i * 32
        for j in range(32):
            row = table[pl.ds(pl.multiple_of(dst_ref[base + j], 2), 2), :]
            got_ref[pl.ds(pl.multiple_of((base + j) * 2, 2), 2), :] = row
        return carry

    lax.fori_loop(0, dst_ref.shape[0] // 32, move, 0)
    out.wait()


def right_call(pieces, kvs, dst, weight):
    split = tuple(len(p) for p in pieces)
    flat = [a for p in pieces for a in p]
    count, run, chans = pieces[0][0].shape
    edges = dst.shape[0]
    rows = sum(a.shape[0] * a.shape[1] for a in flat)
    vmem = pl.BlockSpec(memory_space=pltpu.VMEM)
    return pl.pallas_call(
        functools.partial(right_kernel, split),
        out_shape=(
            jax.ShapeDtypeStruct((count, len(split), run, chans), BF),
            jax.ShapeDtypeStruct((2 * edges, 128), F32),
        ),
        grid_spec=pltpu.PrefetchScalarGridSpec(
            num_scalar_prefetch=2,
            grid=(),
            in_specs=[vmem] * (len(flat) + 1),
            out_specs=(pl.BlockSpec(memory_space=pltpu.HBM), vmem),
            scratch_shapes=[
                pltpu.VMEM((2 * rows, 128), F32),
                pltpu.VMEM((count, len(split), run, chans), BF),
                pltpu.SemaphoreType.DMA,
            ],
        ),
        compiler_params=params(20),
        cost_estimate=pl.CostEstimate(flops=2 * rows * chans * chans, transcendentals=0, bytes_accessed=8 << 20),
        name="right",
    )(kvs, dst, *flat, weight)


def edges_kernel(src_ref, count_ref, left_ref, lower_ref, upper_ref, got_ref, map_ref, out_ref, table, pair_a, pair_b, held, sems):
    ghosts = lower_ref.shape[0]
    own = left_ref.shape[0] - 4 * ghosts
    edges = out_ref.shape[1]
    block = EDGE_BLOCK
    for side, ref in enumerate((lower_ref, upper_ref)):
        store_rows(table, ref[...].astype(F32), [own + side * 2 * ghosts], ghosts)

    def multiply(at, pair):
        for j in range(block):
            a = table[pl.ds(pl.multiple_of(src_ref[at + j], 2), 2), :]
            b = got_ref[pl.ds(pl.multiple_of((at + j) * 2, 2), 2), :]
            pair[2 * j : 2 * j + 2, :] = a * b

    def expand(at, pair):
        total = None
        for half in range(2):
            part = lax.dot_general(
                map_ref[:, half * 128 : half * 128 + 128],
                pair[pl.ds(half, block, stride=2), :].astype(BF),
                (((1,), (1,)), ((), ())),
                preferred_element_type=F32,
            )
            total = part if total is None else total + part
        here = at + lax.broadcasted_iota(jnp.int32, (1, block), 1)
        held[:, pl.ds(pl.multiple_of(at + block, block), block)] = jnp.where(
            here < count_ref[0], total, 0.0
        ).astype(BF)

    def copy_out(i):
        at = pl.multiple_of(i * 2 * block, 2 * block)
        return pltpu.make_async_copy(
            held.at[:, pl.ds(pl.multiple_of(at + block, block), 2 * block)],
            out_ref.at[:, pl.ds(at, 2 * block)],
            sems.at[i],
        )

    turns = edges // (2 * block)

    def turn(i, carry):
        at = i * 2 * block
        expand(at - block, pair_b)
        multiply(at, pair_a)
        expand(at, pair_a)
        multiply(at + block, pair_b)

        @pl.when(i > 0)
        def _():
            copy_out(i - 1).start()

        return carry

    lax.fori_loop(0, turns, turn, 0)
    expand(edges - block, pair_b)
    copy_out(turns - 1).start()
    for i in range(turns):
        copy_out(i).wait()


def edges_call(src, count, left, lower, upper, got, mapping):
    edges = src.shape[0]
    orb = mapping.shape[0]
    vmem = pl.BlockSpec(memory_space=pltpu.VMEM)
    out, _ = pl.pallas_call(
        edges_kernel,
        out_shape=(
            jax.ShapeDtypeStruct((orb, edges), BF),
            jax.ShapeDtypeStruct(left.shape, F32),
        ),
        grid_spec=pltpu.PrefetchScalarGridSpec(
            num_scalar_prefetch=2,
            grid=(),
            in_specs=[vmem] * 5,
            out_specs=(pl.BlockSpec(memory_space=pltpu.HBM), vmem),
            scratch_shapes=[
                pltpu.VMEM((2 * EDGE_BLOCK, 128), F32),
                pltpu.VMEM((2 * EDGE_BLOCK, 128), F32),
                pltpu.VMEM((orb, edges + EDGE_BLOCK), BF),
                pltpu.SemaphoreType.DMA((edges // (2 * EDGE_BLOCK),)),
            ],
        ),
        input_output_aliases={2: 1},
        compiler_params=params(16),
        cost_estimate=pl.CostEstimate(flops=2 * edges * 256 * orb, transcendentals=0, bytes_accessed=8 << 20),
        name="edges",
    )(src, count, left, lower, upper, got, mapping)
    return out


def exchange(pieces, axes):
    return lax.all_to_all(pieces, axes, 0, 0, tiled=True)


def shift(value, axis, by):
    count = lax.axis_size(axis)
    return lax.ppermute(value, axis, [(i, (i + by) % count) for i in range(count)])


def local(
    particle_traits,
    particle_coordinates,
    kspace_vectors,
    learned_kspace_filter,
    spatial_home,
    following_halo_lines,
    previous_halo_lines,
    sender_projection,
    receiver_projection,
    pair_channel_mapping,
    vertex_rescaling_gain,
    link_sender_line,
    link_receiver_particle,
    active_link_tally,
):
    n_atoms = lax.axis_size(ATOM_AXES)
    n_planes = lax.axis_size(PLANE_AXES)
    n_x = lax.axis_size("x")
    n_kvec = lax.axis_size(KV_AXES)
    core = lax.axis_index("core")
    x, yl = lax.axis_index("x"), lax.axis_index("yl")
    atoms, chans = particle_traits.shape
    kdev = kspace_vectors.shape[1]
    norm_scale = 1.0 / math.sqrt(atoms * n_atoms * kdev * n_kvec)
    share = atoms // n_kvec
    run = atoms // n_atoms // n_kvec
    piece = kdev // n_atoms
    core_word = core.astype(jnp.int32)[None]

    in_hbm = lambda a: pltpu.with_memory_space_constraint(a, pltpu.HBM)
    keep, send = struct_call(
        core_word,
        in_hbm(particle_coordinates),
        in_hbm(kspace_vectors),
        in_hbm(particle_traits),
        n_planes,
    )
    chip = (keep.astype(F32) + shift(send, "core", 1).astype(F32)).astype(BF)
    spread = exchange(chip, PLANE_AXES)

    home = spatial_home[0]
    goal = home // run % n_kvec
    tile = (1 - (goal // n_x + yl) % 2) * n_x + (goal - x + 2) % n_x
    own_tile = n_x + 2
    places = tile * share + home // (run * n_kvec) * run + home % run
    want = (places - own_tile * share)[None, :]
    ordered, krhs = order_call(places, core_word, particle_coordinates, kspace_vectors)
    feats = pick_call(want, in_hbm(particle_traits), share)

    struct = jnp.sum(spread.astype(F32), axis=0)
    at = (core * n_planes + lax.axis_index(PLANE_AXES)) * piece
    filter_piece = lax.dynamic_slice_in_dim(learned_kspace_filter, at, piece, 0)
    filtered = (filter_piece[None] * struct * norm_scale).astype(BF)
    own = exchange(jnp.broadcast_to(filtered[None], (n_planes,) + filtered.shape), PLANE_AXES)
    other = shift(own, "core", 1)

    def towards(dy, dx):
        return update_call((1 - dy) * n_x + (dx + 2) % n_x, ordered, krhs, own, other)

    middle = share // 2
    far_across = shift(towards(1, 2), "yl", 1)
    before_across = shift(towards(1, -1), "yl", 1)
    after_across = shift(towards(1, 1), "x", 1)
    far_first, far_second = merge_call(
        towards(0, 2), ((far_across, 0),), (middle, share - middle)
    )
    far_first = shift(far_first, "x", 1)
    far_second = shift(far_second, "x", -1)
    (whole_across,) = merge_call(towards(1, 0), ((after_across, 0),), (share,))
    whole_across = shift(whole_across, "yl", 1)
    (whole_after,) = merge_call(towards(0, 1), ((far_first, 0),), (share,))
    whole_after = shift(whole_after, "x", 1)
    (whole_before,) = merge_call(
        towards(0, -1), ((before_across, 0), (far_second, middle)), (share,)
    )
    whole_before = shift(whole_before, "x", -1)
    parts = [towards(0, 0), whole_across, whole_after, whole_before]
    node = node_call(parts, feats, vertex_rescaling_gain[None, :])
    mine = exchange(node.reshape(n_atoms, run, chans), ATOM_AXES)

    half = n_atoms // 2
    across = shift(mine, "yl", 1)
    before = shift(mine, "x", 1)
    after = shift(mine, "x", -1)
    far = (shift(before[:half], "x", 1), shift(after[half:], "x", -1))
    across_before = shift(across, "x", 1)
    across_after = shift(across, "x", -1)
    across_far = tuple(shift(a, "yl", 1) for a in far)
    pieces = ((mine,), (after,), far, (before,), (across,), (across_after,), across_far, (across_before,))
    offsets = jnp.arange(n_kvec, dtype=jnp.int32)
    kvs = (yl + offsets // n_x) % 2 * n_x + (x + offsets % n_x) % n_x

    ids = jnp.concatenate([following_halo_lines[0], previous_halo_lines[0]]) * 2
    left, for_next, for_previous = halo_call(pieces, kvs, ids, sender_projection)
    lower = shift(for_next, ATOM_AXES, 1)
    upper = shift(for_previous, ATOM_AXES, -1)
    partition_rows, got = right_call(pieces, kvs, link_receiver_particle * 2, receiver_projection)
    orbital_blocks = edges_call(
        link_sender_line * 2, active_link_tally, left, lower, upper, got, pair_channel_mapping
    )
    return (orbital_blocks, partition_rows.reshape(atoms, chans))


def solution(mesh):
    fine = Mesh(mesh.devices.reshape(8, 2, 2, 2, 4), ATOM_AXES + KV_AXES)
    every = ATOM_AXES + KV_AXES
    placed = (
        P(ATOM_AXES, None),
        P(None, ATOM_AXES),
        P(None, KV_AXES),
        P(KV_AXES, None),
        P(ATOM_AXES, None),
        P(ATOM_AXES, None),
        P(ATOM_AXES, None),
        P(),
        P(),
        P(),
        P(),
        P(every),
        P(every),
        P(every),
    )
    return jax.shard_map(
        local,
        mesh=fine,
        in_specs=placed,
        out_specs=(P(None, every), P(ATOM_AXES, None)),
        check_vma=False,
    )
```
